32 devices in a mesh: blk: 16 (over z, y, x), rep: 2 (over core).
Axes of the slice: x: 2, y: 2, z: 4, core: 2. Of those that a mesh axis runs over, the one named last changes fastest.
Arguments:
- entity: bfloat16 [8192, 512], P('blk'), may hold values from -1.1953125 to 1.1953125
- relation: bfloat16 [8, 512, 512], P('rep'), may hold values from -0.25 to 0.25
- head_owner: int32 [8192, 1], P(('blk', 'rep')), may hold values from 0 to 15; in each aligned block of 256 rows (0 to 255, 256 to 511, ...) at most 32 rows name the same one
- head_row: int32 [8192], P(('blk', 'rep')), may hold values from 0 to 511
- query_rel: int32 [8192, 4], P(('blk', 'rep')), may hold values from 0 to 3
- tail_row: int32 [8192, 4], P(('blk', 'rep')), may hold values from 0 to 511
- neg_row: int32 [16, 512], P('blk', 'rep'), may hold values from 0 to 511
Outputs:
- grad_entity: float32 [8192, 512], P('blk', 'rep')
- grad_rel: float32 [8, 512, 512], P('rep', 'blk')
The draws below stay inside these ranges and needn't reach their ends.
Inputs may be any that keep to these rules, and one draw needn't show every extreme that they name: `head_owner`: in each aligned block of 256 rows (the heads of one group) no shard number appears more than 32 times.
All inputs are finite; a program needn't handle non-finite values.
Results may differ from the reference program's by a relative error of at most 0.0035.
Values may be sent and summed in bfloat16 or wider, within the bound.
No kernel may reach another device: no remote copies, remote signals or barrier semaphores. Data moves between devices by JAX's collectives and lax.ppermute only.
A program may use at most 64 MiB of HBM per device.

```python
import math
import jax
import jax.numpy as jnp
import numpy as np
from jax import lax

D = 512
ENT_DEV = 512
HEAD_DEV = 256
QPH = 4
REL_DEV = 4
NEG_ROWS = 256
STOPS = 6
SHARDS = 16
GROUPS = 2
NENT = 8192
REL = 8
HEADS = 8192
CAP = 32
FWD = 3
BACK = 2


def touch_ends(values, own_key, low, high):
    index_at = [jax.random.randint(jax.random.fold_in(own_key, axis), (), 0, length) for axis, length in enumerate(values.shape)]
    widest = values.shape.index(max(values.shape))
    beside = index_at[:widest] + [(index_at[widest] + 1) % values.shape[widest]] + index_at[widest + 1:]
    return values.at[tuple(index_at)].set(low).at[tuple(beside)].set(high)


def level_of(rng, shape, cuts, least, largest):
    def one(axis_at, parts):
        heights = jax.random.uniform(jax.random.fold_in(jax.random.fold_in(rng, 6), axis_at), (parts,), jnp.float32, least / len(cuts), largest / len(cuts))
        return jnp.repeat(jnp.exp(heights), shape[axis_at] // parts).reshape((-1,) + (1,) * (len(shape) - axis_at - 1))

    level = one(*cuts[0])
    for cut in cuts[1:]:
        level = level * one(*cut)
    return level


def deal_out(stream_key, own, number, rows, count, top, bound, slope):
    sequence = jax.random.permutation(stream_key, count)
    packed, ordinary = shares(count, rows * top, bound, slope, True), shares(count, rows * top, bound, slope, False)
    places = jnp.arange(count)

    def named(lengths, offset_by):
        used = int((lengths > 0).sum())
        fixed = max(1, used // 4)
        moved = fixed + (places - fixed + offset_by * (used - fixed)) % max(1, count - fixed)
        return jnp.zeros((count,), jnp.int32).at[sequence[jnp.where(places < fixed, places, moved)]].set(jnp.asarray(lengths, jnp.int32))

    lengths = jnp.where(number % 4 == 0, named(packed, number // 4), named(ordinary, number - number // 4 - 1))
    mixed = jax.random.permutation(jax.random.fold_in(own, 3), count)
    giver, sink = mixed[0:count // 2 * 2:2], mixed[1:count // 2 * 2:2]
    room = jnp.minimum(lengths[giver] - 1, bound - lengths[sink]) // 2
    room = jnp.where((giver == sequence[0]) | (sink == sequence[0]) | (lengths[sink] == 0), 0, jnp.maximum(room, 0))
    moved = jax.random.randint(jax.random.fold_in(own, 4), (count // 2,), 0, 1 << 20) % (room + 1)
    lengths = lengths.at[giver].add(-moved).at[sink].add(moved)
    items = jnp.searchsorted(jnp.cumsum(lengths), jnp.arange(rows * top), side="right").astype(jnp.int32)
    table = items.reshape(top, rows).T
    table = table[jax.random.permutation(jax.random.fold_in(own, 1), rows)]
    offset_by = jax.random.randint(jax.random.fold_in(own, 2), (rows, 1), 0, top)
    return jnp.take_along_axis(table, (jnp.arange(top)[None, :] + offset_by) % top, axis=1)


def shares(number_of, total, bound, slope, full):
    portions = [(1 << 20) // math.isqrt(rank ** slope) + 1 for rank in range(1, number_of + 1)]
    largest = bound if full else min(bound, max(-(-total // number_of), total * portions[0] // sum(portions)))
    least = 1 if total - largest >= number_of - 1 else 0
    given, rest = [largest] + [least] * (number_of - 1), total - largest - least * (number_of - 1)
    while rest > 0:
        candidates = [i for i in range(1, number_of) if given[i] < largest] or [i for i in range(1, number_of) if given[i] < bound]
        mass, remaining = sum([portions[i] for i in candidates]), rest
        for i in candidates:
            extra = min(bound - given[i], max(1, remaining * portions[i] // mass), rest)
            given[i] = given[i] + extra
            rest = rest - extra
    return np.array(given)


def noise(key, shape, spread, limit, cuts=(), held_as=jnp.bfloat16):
    result = jax.random.normal(key, shape, jnp.float32) * spread
    if len(cuts) > 0:
        result = level_of(key, shape, cuts, -0.22, 0.18) * result
    return jnp.clip(result, min=-limit, max=limit).astype(held_as)


def setup_inputs(seed: int = 0) -> dict:
    keys = jax.random.split(jax.random.key(seed), 8)
    entity = noise(keys[0], (NENT, D), 0.2, 1.1953125, ((0, 16),))
    relation = noise(keys[1], (REL, D, D), D ** -0.5, 0.25, ((0, 2),))
    head_owner_keys = jax.random.split(jax.random.fold_in(keys[2], 1), HEADS // HEAD_DEV)
    head_owner_turns = jax.random.permutation(jax.random.fold_in(keys[2], 3), HEADS // HEAD_DEV)
    head_owner = jax.vmap(lambda own, number: deal_out(jax.random.fold_in(keys[2], 2), own, number, HEAD_DEV, SHARDS, 1, CAP, 2))(head_owner_keys, head_owner_turns).reshape((HEADS, 1))
    head_row = touch_ends(jax.random.randint(keys[3], (HEADS,), 0, ENT_DEV), jax.random.fold_in(keys[3], 1), 0, ENT_DEV - 1).astype(jnp.int32)
    query_rel = touch_ends(jax.random.randint(keys[4], (HEADS, QPH), 0, REL_DEV), jax.random.fold_in(keys[4], 1), 0, REL_DEV - 1).astype(jnp.int32)
    tail_row = touch_ends(jax.random.randint(keys[5], (HEADS, QPH), 0, ENT_DEV), jax.random.fold_in(keys[5], 1), 0, ENT_DEV - 1).astype(jnp.int32)
    neg_row = touch_ends(jax.random.randint(keys[6], (SHARDS, GROUPS * NEG_ROWS), 0, ENT_DEV), jax.random.fold_in(keys[6], 1), 0, ENT_DEV - 1).astype(jnp.int32)
    return dict(entity=entity, relation=relation, head_owner=head_owner, head_row=head_row, query_rel=query_rel, tail_row=tail_row, neg_row=neg_row)


def reference(entity, relation, head_owner, head_row, query_rel, tail_row, neg_row):
    group_total = SHARDS * GROUPS
    heads_all = (head_owner[:, 0] * ENT_DEV + head_row).astype(jnp.int32).reshape(group_total, HEAD_DEV)
    rel_all = query_rel.reshape(group_total, HEAD_DEV, QPH)
    tail_all = tail_row.reshape(group_total, HEAD_DEV, QPH)
    shard_base = (jnp.arange(SHARDS, dtype=jnp.int32) * ENT_DEV)[:, None, None]
    neg_ids = (neg_row.reshape(SHARDS, GROUPS, NEG_ROWS) + shard_base).astype(jnp.int32)

    def group_step(state_pair, inputs):
        grad_table, grad_rel = state_pair
        group_index, head_ids, rel_ids, tail_local = inputs
        shard_index = group_index // GROUPS
        rel_group = group_index % GROUPS
        head_vec = jnp.take(entity, head_ids, axis=0)
        rel_mats = lax.dynamic_slice_in_dim(relation, (rel_group * REL_DEV).astype(jnp.int32), REL_DEV, 0)
        queries = jnp.zeros((HEAD_DEV, QPH, D), jnp.float32)
        for rel_index in range(REL_DEV):
            product = jnp.dot(head_vec, rel_mats[rel_index], preferred_element_type=jnp.float32)
            queries = queries + jnp.where((rel_ids == rel_index)[:, :, None], product[:, None, :], 0.0)
        queries = queries.astype(jnp.bfloat16).reshape(HEAD_DEV * QPH, D)
        tail_ids = (shard_index * ENT_DEV + tail_local).reshape(-1).astype(jnp.int32)
        tail_vec = jnp.take(entity, tail_ids, axis=0)
        pos_score = jnp.sum(queries.astype(jnp.float32) * tail_vec.astype(jnp.float32), axis=1)
        pos_weight = jax.nn.sigmoid(pos_score) - 1.0
        grad_query = pos_weight[:, None] * tail_vec.astype(jnp.float32)
        grad_table = grad_table.at[tail_ids].add(pos_weight[:, None] * queries.astype(jnp.float32))
        for offset in range(-BACK, FWD + 1):
            owner_shard = (shard_index - offset) % SHARDS
            block_ids = neg_ids[owner_shard, rel_group]
            neg_block = jnp.take(entity, block_ids, axis=0)
            neg_score = jnp.dot(queries, neg_block.T, preferred_element_type=jnp.float32)
            neg_weight = (jax.nn.sigmoid(neg_score) / STOPS).astype(jnp.bfloat16)
            grad_query = grad_query + jnp.dot(neg_weight, neg_block, preferred_element_type=jnp.float32)
            grad_table = grad_table.at[block_ids].add(jnp.dot(neg_weight.T, queries, preferred_element_type=jnp.float32))
        grad_query = grad_query.reshape(HEAD_DEV, QPH, D)
        grad_head = jnp.zeros((HEAD_DEV, D), jnp.float32)
        for rel_index in range(REL_DEV):
            grad_pair = jnp.sum(jnp.where((rel_ids == rel_index)[:, :, None], grad_query, 0.0), axis=1).astype(jnp.bfloat16)
            grad_head = grad_head + jnp.dot(grad_pair, rel_mats[rel_index].T, preferred_element_type=jnp.float32)
            grad_rel = grad_rel.at[rel_group * REL_DEV + rel_index].add(jnp.dot(head_vec.T, grad_pair, preferred_element_type=jnp.float32))
        grad_table = grad_table.at[head_ids].add(grad_head)
        return (grad_table, grad_rel), None

    start = (jnp.zeros((NENT, D), jnp.float32), jnp.zeros((REL, D, D), jnp.float32))
    groups_iota = jnp.arange(group_total, dtype=jnp.int32)
    final, unused = lax.scan(group_step, start, (groups_iota, heads_all, rel_all, tail_all))
    return final[0], final[1]
```

```python
import functools

import jax
import jax.numpy as jnp
from jax import lax
from jax.experimental import pallas as pl
from jax.experimental.pallas import tpu as pltpu
from jax.sharding import PartitionSpec as P

STOPS = 6
FORE = STOPS // 2
BACK = STOPS - 1 - FORE
OFFSETS = tuple(range(1, FORE + 1)) + tuple(range(-1, -BACK - 1, -1))
BF = jnp.bfloat16
F32 = jnp.float32


def iota(shape, dim):
    return lax.broadcasted_iota(jnp.int32, shape, dim)


def column(row):
    n = row.shape[1]
    return jnp.sum(
        jnp.where(iota((n, n), 0) == iota((n, n), 1), row.astype(F32), 0.0), axis=1, keepdims=True
    ).astype(jnp.int32)


def hot(index, shape, dim):
    return jnp.where(iota(shape, dim) == index, 1.0, 0.0).astype(BF)


def dot(a, b):
    return jnp.dot(a, b, preferred_element_type=F32)


def dot_t(a, b):
    return lax.dot_general(a, b, (((1,), (1,)), ((), ())), preferred_element_type=F32)


def t_dot(a, b):
    return lax.dot_general(a, b, (((0,), (0,)), ((), ())), preferred_element_type=F32)


def halves(x):
    top = x.astype(BF)
    return top, (x - top.astype(F32)).astype(BF)


def ask_kernel(owner_ref, row_ref, asked_ref, pos_ref):
    shards, cap = asked_ref.shape
    heads = owner_ref.shape[1]
    owner = owner_ref[...]
    owner_col = column(owner)
    square = (heads, heads)
    same = owner_col == owner
    slot_row = jnp.sum(
        jnp.where(same & (iota(square, 0) < iota(square, 1)), 1.0, 0.0), axis=0, keepdims=True
    ).astype(jnp.int32)
    slot_col = jnp.sum(
        jnp.where(same & (iota(square, 1) < iota(square, 0)), 1.0, 0.0), axis=1, keepdims=True
    ).astype(jnp.int32)
    pos_ref[...] = owner * cap + slot_row
    value = row_ref[...] + 1
    mine = iota((shards, heads), 0) == owner
    high = jnp.where(mine, (value // 256).astype(F32), 0.0).astype(BF)
    low = jnp.where(mine, (value % 256).astype(F32), 0.0).astype(BF)
    place = hot(slot_col, (heads, cap), 1)
    asked_ref[...] = (256.0 * dot(high, place) + dot(low, place)).astype(jnp.int32) - 1


def take_kernel(row_ref, entity_ref, out_ref):
    count = row_ref.shape[1]
    pick = hot(column(row_ref[...]), (count, entity_ref.shape[0]), 1)
    out_ref[...] = dot(pick, entity_ref[...]).astype(BF)


def serve_kernel(wanted_ref, entity_ref, out_ref):
    shards, cap = wanted_ref.shape
    cols = jnp.concatenate([column(wanted_ref[s : s + 1, :]) for s in range(shards)], axis=0)
    pick = hot(cols, (shards * cap, entity_ref.shape[0]), 1)
    out_ref[...] = dot(pick, entity_ref[...]).astype(BF)


def visit_kernel(pos_ref, qrel_ref, tail_ref, fetched_ref, rel_ref, ent_ref, *refs):
    blocks = refs[:STOPS]
    terms = refs[STOPS : 2 * STOPS]
    vec_ref, q_ref, pw_ref, pair_ref, prod, near, weight, gq = refs[2 * STOPS :]
    heads, width = vec_ref.shape
    rels = rel_ref.shape[0]
    per = qrel_ref.shape[0]
    slots = fetched_ref.shape[0]
    rows = blocks[0].shape[0]
    ents = ent_ref.shape[0]
    for index, block in enumerate(blocks):
        near[index * rows : (index + 1) * rows, :] = block[...]
    vec = dot(hot(column(pos_ref[...]), (heads, slots), 1), fetched_ref[...]).astype(BF)
    vec_ref[...] = vec

    @pl.loop(0, rels)
    def _(k):
        prod[k] = dot(vec_ref[...], rel_ref[k])

    @pl.loop(0, per)
    def _(j):
        kind = column(qrel_ref[pl.ds(j, 1), :])
        query = prod[0]
        for k in range(1, rels):
            query = jnp.where(kind == k, prod[k], query)
        query = query.astype(BF)
        q_ref[j] = query
        tail = dot(hot(column(tail_ref[pl.ds(j, 1), :]), (heads, ents), 1), ent_ref[...])
        score = jnp.sum(query.astype(F32) * tail, axis=1, keepdims=True)
        pw = jax.nn.sigmoid(score) - 1.0
        pw_ref[j] = pw
        seen = dot_t(query, near[...])
        w = (jax.nn.sigmoid(seen) / STOPS).astype(BF)
        weight[pl.ds(pl.multiple_of(j * heads, heads), heads), :] = w
        gq[j] = pw * tail + dot(w, near[...])

    for index, term in enumerate(terms):
        part = t_dot(
            weight[:, index * rows : (index + 1) * rows], q_ref[...].reshape(per * heads, width)
        )
        term[...] = part.astype(term.dtype)
    kinds = [column(qrel_ref[j : j + 1, :]) for j in range(per)]

    @pl.loop(0, rels)
    def _(k):
        total = jnp.where(kinds[0] == k, gq[0], 0.0)
        for j in range(1, per):
            total = total + jnp.where(kinds[j] == k, gq[j], 0.0)
        pair_ref[k] = total.astype(BF)


def push_kernel(
    step, me_ref, pos_ref, vec_ref, pair_ref, rel_ref, keep_a, send_a, keep_b, send_b, bucket_ref, turned, a_side, b_side
):
    heads, width = vec_ref.shape
    rels = rel_ref.shape[0]
    half = width // 2
    slots = bucket_ref.shape[0]
    me = me_ref[0]
    x, y = me % 2, (me // 2) % 2
    turned[...] = vec_ref[...].astype(F32).T
    deep = a_side.shape[0] // 4
    lines = deep // step
    for fx in range(2):
        for fy in range(2):
            for z in range(lines):
                block = z * 4 + ((y + fy) % 2) * 2 + (x + fx) % 2
                rows = turned[pl.ds(pl.multiple_of(block * step, step), step), :]
                at = (fx * 2 + fy) * deep + z * step
                bt = (fy * 2 + fx) * deep + z * step
                a_side[at : at + step, :] = rows
                b_side[bt : bt + step, :] = rows
    head = jnp.zeros((heads, width), F32)
    for k in range(rels):
        head = head + dot_t(pair_ref[k], rel_ref[k])
    bucket_ref[...] = dot(hot(pos_ref[...], (slots, heads), 0), head.astype(BF)).astype(BF)
    for side, keep, send, first in ((a_side, keep_a, send_a, 0), (b_side, keep_b, send_b, rels // 2)):
        for k in range(rels // 2):
            full = dot(side[...].astype(BF), pair_ref[first + k])
            keep[k] = full[:half]
            send[k] = full[half:].astype(BF)


def tail_kernel(tail_ref, q_ref, pw_ref, out_ref):
    ents, heads = out_ref.shape[0], q_ref.shape[1]
    total = jnp.zeros(out_ref.shape, F32)
    for j in range(q_ref.shape[0]):
        spot = hot(tail_ref[j : j + 1, :], (ents, heads), 0)
        top, rest = halves(pw_ref[j] * q_ref[j].astype(F32))
        total = total + dot(spot, top) + dot(spot, rest)
    out_ref[...] = total


def sum_kernel(reps, me_ref, wanted_ref, neg_ref, returned_ref, base_ref, *refs):
    terms = refs[:STOPS]
    own_ref, outs = refs[STOPS], refs[STOPS + 1 :]
    ents = base_ref.shape[0]
    total = terms[0][...]
    for term in terms[1:]:
        total = total + term[...].astype(F32)
    top, rest = halves(total)
    spot = hot(neg_ref[...], (ents, neg_ref.shape[1]), 0)
    back = hot(wanted_ref[...], (ents, wanted_ref.shape[1]), 0)
    full = base_ref[...] + dot(back, returned_ref[...]) + dot(spot, top) + dot(spot, rest)
    chunk = own_ref.shape[1]
    rep = me_ref[1]
    parts = [full[:, c * chunk : (c + 1) * chunk] for c in range(reps)]

    def pick(number):
        value = parts[0]
        for c in range(1, reps):
            value = jnp.where(number == c, parts[c], value)
        return value

    own_ref[...] = pick(rep)
    for shift, out in enumerate(outs):
        out[...] = pick((rep + shift + 1) % reps).astype(BF)


def kernel(body, outs, scratch=(), smem=0):
    def call(*args):
        specs = [
            pl.BlockSpec(memory_space=pltpu.SMEM if i < smem else pltpu.VMEM) for i in range(len(args))
        ]
        return pl.pallas_call(
            body,
            out_shape=[jax.ShapeDtypeStruct(s, d) for s, d in outs],
            in_specs=specs,
            out_specs=[pl.BlockSpec(memory_space=pltpu.VMEM)] * len(outs),
            scratch_shapes=[pltpu.VMEM(s, d) for s, d in scratch],
        )(*args)

    return call


def per_device(entity, relation, head_owner, head_row, query_rel, tail_row, neg_row):
    shards, reps = lax.axis_size("blk"), lax.axis_size("rep")
    ents, width = entity.shape
    rels = relation.shape[0]
    heads = head_row.shape[0]
    per = query_rel.shape[1]
    rows = neg_row.shape[1]
    cap = max(2, 2 * heads // shards)
    slots = shards * cap
    step = width // shards
    lines = shards // 4
    me = jnp.stack([lax.axis_index("blk"), lax.axis_index("rep")]).astype(jnp.int32)

    owner_row = head_owner.reshape(1, heads)
    qrel, tail = query_rel.T, tail_row.T
    asked, pos = kernel(ask_kernel, [((shards, cap), jnp.int32), ((1, heads), jnp.int32)])(
        owner_row, head_row.reshape(1, heads)
    )
    wanted = lax.all_to_all(asked, "blk", split_axis=0, concat_axis=0, tiled=True)
    (own_block,) = kernel(take_kernel, [((rows, width), BF)])(neg_row, entity)

    def moved(value, distance):
        return lax.ppermute(value, "blk", [((i - distance) % shards, i) for i in range(shards)])

    def flipped(value, bit):
        return lax.ppermute(value, "blk", [(i, i ^ bit) for i in range(shards)])

    blocks = [own_block] + [moved(own_block, o) for o in OFFSETS]
    (served,) = kernel(serve_kernel, [((slots, width), BF)])(wanted, entity)
    fetched = lax.all_to_all(
        served.reshape(shards, cap, width), "blk", split_axis=0, concat_axis=0, tiled=True
    ).reshape(slots, width)

    outs = [((rows, width), F32)] + [((rows, width), BF)] * (STOPS - 1)
    outs += [((heads, width), BF), ((per, heads, width), BF), ((per, heads, 1), F32), ((rels, heads, width), BF)]
    scratch = [
        ((rels, heads, width), F32),
        ((STOPS * rows, width), BF),
        ((per * heads, STOPS * rows), BF),
        ((per, heads, width), F32),
    ]
    *terms, vec, queries, pos_weight, pair = kernel(visit_kernel, outs, scratch)(
        pos, qrel, tail, fetched, relation, entity, *blocks
    )
    back = [terms[0]] + [moved(t, -o) for t, o in zip(terms[1:], OFFSETS)]

    part = (rels // 2, width // 2, width)
    keep_a, send_a, keep_b, send_b, buckets = kernel(
        functools.partial(push_kernel, step),
        [(part, F32), (part, BF), (part, F32), (part, BF), ((slots, width), BF)],
        [((width, heads), F32)] * 3,
        smem=1,
    )(me, pos, vec, pair, relation)
    got_a, got_b = flipped(send_a, 1), flipped(send_b, 2)
    returned = lax.all_to_all(
        buckets.reshape(shards, cap, width), "blk", split_axis=0, concat_axis=0, tiled=True
    ).reshape(slots, width)
    (base,) = kernel(tail_kernel, [((ents, width), F32)])(tail, queries, pos_weight)

    quarter = width // 4
    sum_a = keep_a + got_a.astype(F32)
    sum_b = keep_b + got_b.astype(F32)
    more_a = flipped(sum_a[:, quarter:].astype(BF), 2)
    more_b = flipped(sum_b[:, quarter:].astype(BF), 1)
    sum_a = sum_a[:, :quarter] + more_a.astype(F32)
    sum_b = sum_b[:, :quarter] + more_b.astype(F32)
    both = jnp.concatenate([sum_a, sum_b]).astype(BF).reshape(rels, lines, step, width)
    both = both.transpose(1, 0, 2, 3)
    groups = [[c + 4 * z for z in range(lines)] for c in range(4)]
    lined = lax.all_to_all(
        both, "blk", split_axis=0, concat_axis=0, tiled=True, axis_index_groups=groups
    )
    grad_rel = jnp.sum(lined.astype(F32), axis=0)

    chunk = width // reps
    own, *others = kernel(
        functools.partial(sum_kernel, reps),
        [((ents, chunk), F32)] + [((ents, chunk), BF)] * (reps - 1),
        smem=1,
    )(me, wanted.reshape(1, slots), neg_row, returned, base, *back)
    grad_entity = own
    for shift, other in enumerate(others):
        route = [(i, (i + shift + 1) % reps) for i in range(reps)]
        grad_entity = grad_entity + lax.ppermute(other, "rep", route).astype(F32)
    return (grad_entity, grad_rel)


def solution(mesh):
    placed = (
        P("blk", None),
        P("rep", None, None),
        P(("blk", "rep"), None),
        P(("blk", "rep")),
        P(("blk", "rep"), None),
        P(("blk", "rep"), None),
        P("blk", "rep"),
    )
    return jax.shard_map(
        per_device,
        mesh=mesh,
        in_specs=placed,
        out_specs=(P("blk", "rep"), P("rep", "blk", None)),
        check_vma=False,
    )
```

```python
import functools

import jax
import jax.numpy as jnp
from jax import lax
from jax.experimental import pallas as pl
from jax.experimental.pallas import tpu as pltpu
from jax.sharding import PartitionSpec as P


STOPS = 6
FORE = STOPS // 2
BACK = STOPS - 1 - FORE
OFFSETS = tuple(range(1, FORE + 1)) + tuple(range(-1, -BACK - 1, -1))
BF = jnp.bfloat16
F32 = jnp.float32


def iota(shape, dim):
    return lax.broadcasted_iota(jnp.int32, shape, dim)


def column(row):
    n = row.shape[1]
    return jnp.sum(
        jnp.where(iota((n, n), 0) == iota((n, n), 1), row.astype(F32), 0.0), axis=1, keepdims=True
    ).astype(jnp.int32)


def hot(index, shape, dim):
    return jnp.where(iota(shape, dim) == index, 1.0, 0.0).astype(BF)


def dot(a, b):
    return jnp.dot(a, b, preferred_element_type=F32)


def dot_t(a, b):
    return lax.dot_general(a, b, (((1,), (1,)), ((), ())), preferred_element_type=F32)


def t_dot(a, b):
    return lax.dot_general(a, b, (((0,), (0,)), ((), ())), preferred_element_type=F32)


def halves(x):
    top = x.astype(BF)
    return top, (x - top.astype(F32)).astype(BF)


def ask_kernel(owner_ref, row_ref, asked_ref, pos_ref):
    shards, cap = asked_ref.shape
    heads = owner_ref.shape[1]
    owner = owner_ref[...]
    owner_col = column(owner)
    square = (heads, heads)
    same = owner_col == owner
    slot_row = jnp.sum(
        jnp.where(same & (iota(square, 0) < iota(square, 1)), 1.0, 0.0), axis=0, keepdims=True
    ).astype(jnp.int32)
    slot_col = jnp.sum(
        jnp.where(same & (iota(square, 1) < iota(square, 0)), 1.0, 0.0), axis=1, keepdims=True
    ).astype(jnp.int32)
    pos_ref[...] = owner * cap + slot_row
    value = row_ref[...] + 1
    mine = iota((shards, heads), 0) == owner
    high = jnp.where(mine, (value // 256).astype(F32), 0.0).astype(BF)
    low = jnp.where(mine, (value % 256).astype(F32), 0.0).astype(BF)
    place = hot(slot_col, (heads, cap), 1)
    asked_ref[...] = (256.0 * dot(high, place) + dot(low, place)).astype(jnp.int32) - 1


def take_kernel(row_ref, entity_ref, out_ref):
    count = row_ref.shape[1]
    pick = hot(column(row_ref[...]), (count, entity_ref.shape[0]), 1)
    out_ref[...] = dot(pick, entity_ref[...]).astype(BF)


def serve_kernel(wanted_ref, entity_ref, out_ref):
    shards, cap = wanted_ref.shape
    cols = jnp.concatenate([column(wanted_ref[s : s + 1, :]) for s in range(shards)], axis=0)
    pick = hot(cols, (shards * cap, entity_ref.shape[0]), 1)
    out_ref[...] = dot(pick, entity_ref[...]).astype(BF)


def visit_kernel(pos_ref, qrel_ref, tail_ref, fetched_ref, rel_ref, ent_ref, *refs):
    blocks = refs[:STOPS]
    terms = refs[STOPS : 2 * STOPS]
    vec_ref, q_ref, pw_ref, pair_ref, prod, near, weight, gq = refs[2 * STOPS :]
    heads, width = vec_ref.shape
    rels = rel_ref.shape[0]
    per = qrel_ref.shape[0]
    slots = fetched_ref.shape[0]
    rows = blocks[0].shape[0]
    ents = ent_ref.shape[0]
    for index, block in enumerate(blocks):
        near[index * rows : (index + 1) * rows, :] = block[...]
    vec = dot(hot(column(pos_ref[...]), (heads, slots), 1), fetched_ref[...]).astype(BF)
    vec_ref[...] = vec

    @pl.loop(0, rels)
    def _(k):
        prod[k] = dot(vec_ref[...], rel_ref[k])

    @pl.loop(0, per)
    def _(j):
        kind = column(qrel_ref[pl.ds(j, 1), :])
        query = prod[0]
        for k in range(1, rels):
            query = jnp.where(kind == k, prod[k], query)
        query = query.astype(BF)
        q_ref[j] = query
        tail = dot(hot(column(tail_ref[pl.ds(j, 1), :]), (heads, ents), 1), ent_ref[...])
        score = jnp.sum(query.astype(F32) * tail, axis=1, keepdims=True)
        pw = jax.nn.sigmoid(score) - 1.0
        pw_ref[j] = pw
        seen = dot_t(query, near[...])
        w = (jax.nn.sigmoid(seen) / STOPS).astype(BF)
        weight[pl.ds(pl.multiple_of(j * heads, heads), heads), :] = w
        gq[j] = pw * tail + dot(w, near[...])

    for index, term in enumerate(terms):
        part = t_dot(
            weight[:, index * rows : (index + 1) * rows], q_ref[...].reshape(per * heads, width)
        )
        term[...] = part.astype(term.dtype)
    kinds = [column(qrel_ref[j : j + 1, :]) for j in range(per)]

    @pl.loop(0, rels)
    def _(k):
        total = jnp.where(kinds[0] == k, gq[0], 0.0)
        for j in range(1, per):
            total = total + jnp.where(kinds[j] == k, gq[j], 0.0)
        pair_ref[k] = total.astype(BF)


def push_kernel(
    step, me_ref, pos_ref, vec_ref, pair_ref, rel_ref, keep_a, send_a, keep_b, send_b, bucket_ref, turned, a_side, b_side
):
    heads, width = vec_ref.shape
    rels = rel_ref.shape[0]
    half = width // 2
    slots = bucket_ref.shape[0]
    me = me_ref[0]
    x, y = me % 2, (me // 2) % 2
    turned[...] = vec_ref[...].astype(F32).T
    deep = a_side.shape[0] // 4
    lines = deep // step
    for fx in range(2):
        for fy in range(2):
            for z in range(lines):
                block = z * 4 + ((y + fy) % 2) * 2 + (x + fx) % 2
                rows = turned[pl.ds(pl.multiple_of(block * step, step), step), :]
                at = (fx * 2 + fy) * deep + z * step
                bt = (fy * 2 + fx) * deep + z * step
                a_side[at : at + step, :] = rows
                b_side[bt : bt + step, :] = rows
    head = jnp.zeros((heads, width), F32)
    for k in range(rels):
        head = head + dot_t(pair_ref[k], rel_ref[k])
    bucket_ref[...] = dot(hot(pos_ref[...], (slots, heads), 0), head.astype(BF)).astype(BF)
    for side, keep, send, first in ((a_side, keep_a, send_a, 0), (b_side, keep_b, send_b, rels // 2)):
        for k in range(rels // 2):
            full = dot(side[...].astype(BF), pair_ref[first + k])
            keep[k] = full[:half]
            send[k] = full[half:].astype(BF)


def tail_kernel(tail_ref, q_ref, pw_ref, out_ref):
    ents, heads = out_ref.shape[0], q_ref.shape[1]
    total = jnp.zeros(out_ref.shape, F32)
    for j in range(q_ref.shape[0]):
        spot = hot(tail_ref[j : j + 1, :], (ents, heads), 0)
        top, rest = halves(pw_ref[j] * q_ref[j].astype(F32))
        total = total + dot(spot, top) + dot(spot, rest)
    out_ref[...] = total


def sum_kernel(reps, me_ref, wanted_ref, neg_ref, returned_ref, base_ref, *refs):
    terms = refs[:STOPS]
    own_ref, outs = refs[STOPS], refs[STOPS + 1 :]
    ents = base_ref.shape[0]
    total = terms[0][...]
    for term in terms[1:]:
        total = total + term[...].astype(F32)
    top, rest = halves(total)
    spot = hot(neg_ref[...], (ents, neg_ref.shape[1]), 0)
    back = hot(wanted_ref[...], (ents, wanted_ref.shape[1]), 0)
    full = base_ref[...] + dot(back, returned_ref[...]) + dot(spot, top) + dot(spot, rest)
    chunk = own_ref.shape[1]
    rep = me_ref[1]
    parts = [full[:, c * chunk : (c + 1) * chunk] for c in range(reps)]

    def pick(number):
        value = parts[0]
        for c in range(1, reps):
            value = jnp.where(number == c, parts[c], value)
        return value

    own_ref[...] = pick(rep)
    for shift, out in enumerate(outs):
        out[...] = pick((rep + shift + 1) % reps).astype(BF)


def kernel(body, outs, scratch=(), smem=0):
    def call(*args):
        specs = [
            pl.BlockSpec(memory_space=pltpu.SMEM if i < smem else pltpu.VMEM) for i in range(len(args))
        ]
        return pl.pallas_call(
            body,
            out_shape=[jax.ShapeDtypeStruct(s, d) for s, d in outs],
            in_specs=specs,
            out_specs=[pl.BlockSpec(memory_space=pltpu.VMEM)] * len(outs),
            scratch_shapes=[pltpu.VMEM(s, d) for s, d in scratch],
        )(*args)

    return call


def per_device(entity, relation, head_owner, head_row, query_rel, tail_row, neg_row):
    shards, reps = lax.axis_size("blk"), lax.axis_size("rep")
    ents, width = entity.shape
    rels = relation.shape[0]
    heads = head_row.shape[0]
    per = query_rel.shape[1]
    rows = neg_row.shape[1]
    cap = max(2, 2 * heads // shards)
    slots = shards * cap
    step = width // shards
    lines = shards // 4
    me = jnp.stack([lax.axis_index("blk"), lax.axis_index("rep")]).astype(jnp.int32)

    def moved(value, distance):
        return lax.ppermute(value, "blk", [((i - distance) % shards, i) for i in range(shards)])

    def flipped(value, bit):
        return lax.ppermute(value, "blk", [(i, i ^ bit) for i in range(shards)])

    def dealt(value, groups=None):
        return lax.all_to_all(
            value, "blk", split_axis=0, concat_axis=0, tiled=True, axis_index_groups=groups
        )

    owner_row = head_owner.reshape(1, heads)
    qrel, tail = query_rel.T, tail_row.T
    (own_block,) = kernel(take_kernel, [((rows, width), BF)])(neg_row, entity)
    blocks = [own_block] + [moved(own_block, o) for o in OFFSETS]
    asked, pos = kernel(ask_kernel, [((shards, cap), jnp.int32), ((1, heads), jnp.int32)])(
        owner_row, head_row.reshape(1, heads)
    )
    wanted = dealt(asked)
    (served,) = kernel(serve_kernel, [((slots, width), BF)])(wanted, entity)
    fetched = dealt(served.reshape(shards, cap, width)).reshape(slots, width)

    outs = [((rows, width), F32)] + [((rows, width), BF)] * (STOPS - 1)
    outs += [((heads, width), BF), ((per, heads, width), BF), ((per, heads, 1), F32), ((rels, heads, width), BF)]
    scratch = [
        ((rels, heads, width), F32),
        ((STOPS * rows, width), BF),
        ((per * heads, STOPS * rows), BF),
        ((per, heads, width), F32),
    ]
    *terms, vec, queries, pos_weight, pair = kernel(visit_kernel, outs, scratch)(
        pos, qrel, tail, fetched, relation, entity, *blocks
    )
    back = [terms[0]] + [moved(terms[n + 1], -o) for n, o in enumerate(OFFSETS)]

    part = (rels // 2, width // 2, width)
    keep_a, send_a, keep_b, send_b, buckets = kernel(
        functools.partial(push_kernel, step),
        [(part, F32), (part, BF), (part, F32), (part, BF), ((slots, width), BF)],
        [((width, heads), F32)] * 3,
        smem=1,
    )(me, pos, vec, pair, relation)
    got_a = flipped(send_a, 1)
    got_b = flipped(send_b, 2)
    returned = dealt(buckets.reshape(shards, cap, width)).reshape(slots, width)
    (base,) = kernel(tail_kernel, [((ents, width), F32)])(tail, queries, pos_weight)

    quarter = width // 4
    sum_a = keep_a + got_a.astype(F32)
    sum_b = keep_b + got_b.astype(F32)
    next_a, next_b = sum_a[:, quarter:].astype(BF), sum_b[:, quarter:].astype(BF)
    more_a = flipped(next_a, 2)
    more_b = flipped(next_b, 1)
    sum_a = sum_a[:, :quarter] + more_a.astype(F32)
    sum_b = sum_b[:, :quarter] + more_b.astype(F32)
    both = jnp.concatenate([sum_a, sum_b]).astype(BF).reshape(rels, lines, step, width)
    both = both.transpose(1, 0, 2, 3)
    lined = dealt(both, [[c + 4 * z for z in range(lines)] for c in range(4)])
    grad_rel = jnp.sum(lined.astype(F32), axis=0)

    chunk = width // reps
    own, *others = kernel(
        functools.partial(sum_kernel, reps),
        [((ents, chunk), F32)] + [((ents, chunk), BF)] * (reps - 1),
        smem=1,
    )(me, wanted.reshape(1, slots), neg_row, returned, base, *back)
    grad_entity = own
    for shift, other in enumerate(others):
        route = [(i, (i + shift + 1) % reps) for i in range(reps)]
        grad_entity = grad_entity + lax.ppermute(other, "rep", route).astype(F32)
    return (grad_entity, grad_rel)


def solution(mesh):
    placed = (
        P("blk", None),
        P("rep", None, None),
        P(("blk", "rep"), None),
        P(("blk", "rep")),
        P(("blk", "rep"), None),
        P(("blk", "rep"), None),
        P("blk", "rep"),
    )

    return jax.shard_map(
        per_device,
        mesh=mesh,
        in_specs=placed,
        out_specs=(P("blk", "rep"), P("rep", "blk", None)),
        check_vma=False,
    )
```

```python
import functools

import jax
import jax.numpy as jnp
from jax import lax
from jax.experimental import pallas as pl
from jax.experimental.pallas import tpu as pltpu
from jax.sharding import PartitionSpec as P


STOPS = 6
FORE = STOPS // 2
BACK = STOPS - 1 - FORE
OFFSETS = tuple(range(1, FORE + 1)) + tuple(range(-1, -BACK - 1, -1))
VMEM = 24 << 20
BF = jnp.bfloat16
F32 = jnp.float32


def iota(shape, dim):
    return lax.broadcasted_iota(jnp.int32, shape, dim)


def column(row):
    n = row.shape[1]
    return jnp.sum(
        jnp.where(iota((n, n), 0) == iota((n, n), 1), row.astype(F32), 0.0), axis=1, keepdims=True
    ).astype(jnp.int32)


def hot(index, shape, dim):
    return jnp.where(iota(shape, dim) == index, 1.0, 0.0).astype(BF)


def dot(a, b):
    return jnp.dot(a, b, preferred_element_type=F32)


def dot_t(a, b):
    return lax.dot_general(a, b, (((1,), (1,)), ((), ())), preferred_element_type=F32)


def t_dot(a, b):
    return lax.dot_general(a, b, (((0,), (0,)), ((), ())), preferred_element_type=F32)


def halves(x):
    top = x.astype(BF)
    return top, (x - top.astype(F32)).astype(BF)


def ask_kernel(owner_ref, row_ref, asked_ref, pos_ref):
    shards, cap = asked_ref.shape
    heads = owner_ref.shape[1]
    owner = owner_ref[...]
    owner_col = column(owner)
    square = (heads, heads)
    same = owner_col == owner
    slot_row = jnp.sum(
        jnp.where(same & (iota(square, 0) < iota(square, 1)), 1.0, 0.0), axis=0, keepdims=True
    ).astype(jnp.int32)
    slot_col = jnp.sum(
        jnp.where(same & (iota(square, 1) < iota(square, 0)), 1.0, 0.0), axis=1, keepdims=True
    ).astype(jnp.int32)
    pos_ref[...] = owner * cap + slot_row
    value = row_ref[...] + 1
    mine = iota((shards, heads), 0) == owner
    high = jnp.where(mine, (value // 256).astype(F32), 0.0).astype(BF)
    low = jnp.where(mine, (value % 256).astype(F32), 0.0).astype(BF)
    place = hot(slot_col, (heads, cap), 1)
    asked_ref[...] = (256.0 * dot(high, place) + dot(low, place)).astype(jnp.int32) - 1


def take_kernel(row_ref, entity_ref, out_ref):
    count = row_ref.shape[1]
    pick = hot(column(row_ref[...]), (count, entity_ref.shape[0]), 1)
    out_ref[...] = dot(pick, entity_ref[...]).astype(BF)


def serve_kernel(wanted_ref, entity_ref, out_ref):
    shards, cap = wanted_ref.shape
    cols = jnp.concatenate([column(wanted_ref[s : s + 1, :]) for s in range(shards)], axis=0)
    pick = hot(cols, (shards * cap, entity_ref.shape[0]), 1)
    out_ref[...] = dot(pick, entity_ref[...]).astype(BF)


def query_kernel(pos_ref, qrel_ref, fetched_ref, rel_ref, vec_ref, q_ref, prod):
    heads = vec_ref.shape[0]
    rels = rel_ref.shape[0]
    slots = fetched_ref.shape[0]
    vec = dot(hot(column(pos_ref[...]), (heads, slots), 1), fetched_ref[...]).astype(BF)
    vec_ref[...] = vec
    for k in range(rels):
        prod[k] = dot(vec, rel_ref[k])
    for j in range(qrel_ref.shape[0]):
        kind = column(qrel_ref[j : j + 1, :])
        query = prod[0]
        for k in range(1, rels):
            query = jnp.where(kind == k, prod[k], query)
        q_ref[j * heads : (j + 1) * heads, :] = query.astype(BF)


def weigh(q_ref, block_ref, weight, chunk):
    for at in range(0, q_ref.shape[0], chunk):
        seen = dot_t(q_ref[at : at + chunk, :], block_ref[...])
        weight[at : at + chunk, :] = (jax.nn.sigmoid(seen) / STOPS).astype(BF)


def visit_kernel(chunk, q_ref, block_ref, weight, term):
    weigh(q_ref, block_ref, weight, chunk)
    term[...] = t_dot(weight[...], q_ref[...]).astype(term.dtype)


def pair_kernel(q_ref, qrel_ref, tail_ref, ent_ref, own_ref, *refs):
    others = STOPS - 1
    weights, blocks = refs[:others], refs[others : 2 * others]
    pw_ref, pair_ref, term, weight, gq = refs[2 * others :]
    per, heads = qrel_ref.shape
    ents = ent_ref.shape[0]
    weigh(q_ref, own_ref, weight, heads)
    term[...] = t_dot(weight[...], q_ref[...])
    for j in range(per):
        here = slice(j * heads, (j + 1) * heads)
        tail = dot(hot(column(tail_ref[j : j + 1, :]), (heads, ents), 1), ent_ref[...])
        score = jnp.sum(q_ref[here, :].astype(F32) * tail, axis=1, keepdims=True)
        pw = jax.nn.sigmoid(score) - 1.0
        pw_ref[j] = pw
        total = pw * tail + dot(weight[here, :], own_ref[...])
        for one, block in zip(weights, blocks):
            total = total + dot(one[here, :], block[...])
        gq[j] = total
    kinds = [column(qrel_ref[j : j + 1, :]) for j in range(per)]
    for k in range(pair_ref.shape[0]):
        total = jnp.where(kinds[0] == k, gq[0], 0.0)
        for j in range(1, per):
            total = total + jnp.where(kinds[j] == k, gq[j], 0.0)
        pair_ref[k] = total.astype(BF)


def rel_kernel(step, first, outer, me_ref, vec_ref, pair_ref, keep, send, turned, side):
    count, half = keep.shape[:2]
    inner = 1 - outer
    me = me_ref[0]
    bits = (me % 2, (me // 2) % 2)
    turned[...] = vec_ref[...].astype(F32).T
    lines = half // 2 // step
    for flips in range(4):
        flip = (flips // 2, flips % 2)
        bit = [0, 0]
        bit[outer] = (bits[outer] + flip[0]) % 2
        bit[inner] = (bits[inner] + flip[1]) % 2
        for z in range(lines):
            block = z * 4 + bit[1] * 2 + bit[0]
            at = (flips * lines + z) * step
            side[at : at + step, :] = turned[pl.ds(pl.multiple_of(block * step, step), step), :]
    for k in range(count):
        send[k] = dot(side[half:, :].astype(BF), pair_ref[first + k]).astype(BF)
    for k in range(count):
        keep[k] = dot(side[:half, :].astype(BF), pair_ref[first + k])


def head_kernel(pos_ref, pair_ref, rel_ref, bucket_ref):
    rels, heads, _ = pair_ref.shape
    head = dot_t(pair_ref[0], rel_ref[0])
    for k in range(1, rels):
        head = head + dot_t(pair_ref[k], rel_ref[k])
    slots = bucket_ref.shape[0]
    bucket_ref[...] = dot(hot(pos_ref[...], (slots, heads), 0), head.astype(BF)).astype(BF)


def tail_kernel(tail_ref, q_ref, pw_ref, out_ref):
    ents, heads = out_ref.shape[0], tail_ref.shape[1]
    total = jnp.zeros(out_ref.shape, F32)
    for j in range(tail_ref.shape[0]):
        spot = hot(tail_ref[j : j + 1, :], (ents, heads), 0)
        top, rest = halves(pw_ref[j] * q_ref[j * heads : (j + 1) * heads, :].astype(F32))
        total = total + dot(spot, top) + dot(spot, rest)
    out_ref[...] = total


def sum_kernel(reps, me_ref, wanted_ref, neg_ref, returned_ref, base_ref, *refs):
    terms = refs[:STOPS]
    own_ref, outs = refs[STOPS], refs[STOPS + 1 :]
    ents = base_ref.shape[0]
    total = terms[0][...]
    for term in terms[1:]:
        total = total + term[...].astype(F32)
    top, rest = halves(total)
    spot = hot(neg_ref[...], (ents, neg_ref.shape[1]), 0)
    back = hot(wanted_ref[...], (ents, wanted_ref.shape[1]), 0)
    full = base_ref[...] + dot(back, returned_ref[...]) + dot(spot, top) + dot(spot, rest)
    chunk = own_ref.shape[1]
    rep = me_ref[1]
    parts = [full[:, c * chunk : (c + 1) * chunk] for c in range(reps)]

    def pick(number):
        value = parts[0]
        for c in range(1, reps):
            value = jnp.where(number == c, parts[c], value)
        return value

    own_ref[...] = pick(rep)
    for shift, out in enumerate(outs):
        out[...] = pick((rep + shift + 1) % reps).astype(BF)


def kernel(body, outs, scratch=(), smem=0):
    def call(*args):
        specs = [
            pl.BlockSpec(memory_space=pltpu.SMEM if i < smem else pltpu.VMEM) for i in range(len(args))
        ]
        return pl.pallas_call(
            body,
            out_shape=[jax.ShapeDtypeStruct(s, d) for s, d in outs],
            in_specs=specs,
            out_specs=[pl.BlockSpec(memory_space=pltpu.VMEM)] * len(outs),
            scratch_shapes=[pltpu.VMEM(s, d) for s, d in scratch],
            compiler_params=pltpu.CompilerParams(vmem_limit_bytes=VMEM),
        )(*args)

    return call


def per_device(entity, relation, head_owner, head_row, query_rel, tail_row, neg_row):
    shards, reps = lax.axis_size("blk"), lax.axis_size("rep")
    ents, width = entity.shape
    rels = relation.shape[0]
    heads = head_row.shape[0]
    per = query_rel.shape[1]
    rows = neg_row.shape[1]
    cap = max(2, 2 * heads // shards)
    slots = shards * cap
    step = width // shards
    lines = shards // 4
    me = jnp.stack([lax.axis_index("blk"), lax.axis_index("rep")]).astype(jnp.int32)

    def moved(value, distance):
        return lax.ppermute(value, "blk", [((i - distance) % shards, i) for i in range(shards)])

    def flipped(value, bit):
        return lax.ppermute(value, "blk", [(i, i ^ bit) for i in range(shards)])

    def dealt(value, groups=None):
        return lax.all_to_all(
            value, "blk", split_axis=0, concat_axis=0, tiled=True, axis_index_groups=groups
        )

    owner_row = head_owner.reshape(1, heads)
    qrel, tail = query_rel.T, tail_row.T
    (own_block,) = kernel(take_kernel, [((rows, width), BF)])(neg_row, entity)
    blocks = [own_block] + [moved(own_block, o) for o in OFFSETS]
    asked, pos = kernel(ask_kernel, [((shards, cap), jnp.int32), ((1, heads), jnp.int32)])(
        owner_row, head_row.reshape(1, heads)
    )
    wanted = dealt(asked)
    (served,) = kernel(serve_kernel, [((slots, width), BF)])(wanted, entity)
    fetched = dealt(served.reshape(shards, cap, width)).reshape(slots, width)

    many = per * heads
    vec, queries = kernel(
        query_kernel, [((heads, width), BF), ((many, width), BF)], [((rels, heads, width), F32)]
    )(pos, qrel, fetched, relation)
    weights, back = [], []
    for n, offset in enumerate(OFFSETS):
        weight, term = kernel(
            functools.partial(visit_kernel, heads), [((many, rows), BF), ((rows, width), BF)]
        )(queries, blocks[n + 1])
        weights.append(weight)
        back.append(moved(term, -offset))
    pos_weight, pair, own_term = kernel(
        pair_kernel,
        [((per, heads, 1), F32), ((rels, heads, width), BF), ((rows, width), F32)],
        [((many, rows), BF), ((per, heads, width), F32)],
    )(queries, qrel, tail, entity, own_block, *weights, *blocks[1:])
    back = [own_term] + back

    part = (rels // 2, width // 2, width)

    def relations(first, outer):
        return kernel(
            functools.partial(rel_kernel, step, first, outer),
            [(part, F32), (part, BF)],
            [((width, heads), F32)] * 2,
            smem=1,
        )(me, vec, pair)

    keep_a, send_a = relations(0, 0)
    got_a = flipped(send_a, 1)
    keep_b, send_b = relations(rels // 2, 1)
    got_b = flipped(send_b, 2)
    (buckets,) = kernel(head_kernel, [((slots, width), BF)])(pos, pair, relation)
    returned = dealt(buckets.reshape(shards, cap, width)).reshape(slots, width)
    (base,) = kernel(tail_kernel, [((ents, width), F32)])(tail, queries, pos_weight)

    quarter = width // 4
    sum_a = keep_a + got_a.astype(F32)
    sum_b = keep_b + got_b.astype(F32)
    next_a, next_b = sum_a[:, quarter:].astype(BF), sum_b[:, quarter:].astype(BF)
    more_a = flipped(next_a, 2)
    more_b = flipped(next_b, 1)
    sum_a = sum_a[:, :quarter] + more_a.astype(F32)
    sum_b = sum_b[:, :quarter] + more_b.astype(F32)
    both = jnp.concatenate([sum_a, sum_b]).astype(BF).reshape(rels, lines, step, width)
    both = both.transpose(1, 0, 2, 3)
    lined = dealt(both, [[c + 4 * z for z in range(lines)] for c in range(4)])
    grad_rel = jnp.sum(lined.astype(F32), axis=0)

    chunk = width // reps
    own, *others = kernel(
        functools.partial(sum_kernel, reps),
        [((ents, chunk), F32)] + [((ents, chunk), BF)] * (reps - 1),
        smem=1,
    )(me, wanted.reshape(1, slots), neg_row, returned, base, *back)
    grad_entity = own
    for shift, other in enumerate(others):
        route = [(i, (i + shift + 1) % reps) for i in range(reps)]
        grad_entity = grad_entity + lax.ppermute(other, "rep", route).astype(F32)
    return (grad_entity, grad_rel)


def solution(mesh):
    placed = (
        P("blk", None),
        P("rep", None, None),
        P(("blk", "rep"), None),
        P(("blk", "rep")),
        P(("blk", "rep"), None),
        P(("blk", "rep"), None),
        P("blk", "rep"),
    )

    return jax.shard_map(
        per_device,
        mesh=mesh,
        in_specs=placed,
        out_specs=(P("blk", "rep"), P("rep", "blk", None)),
        check_vma=False,
    )
```

```python
import functools

import jax
import jax.numpy as jnp
from jax import lax
from jax.experimental import pallas as pl
from jax.experimental.pallas import tpu as pltpu
from jax.sharding import PartitionSpec as P


STOPS = 6
FORE = STOPS // 2
BACK = STOPS - 1 - FORE
OFFSETS = tuple(range(1, FORE + 1)) + tuple(range(-1, -BACK - 1, -1))
VMEM = 12 << 20
BF = jnp.bfloat16
F32 = jnp.float32
VM, HM = pltpu.VMEM, pltpu.HBM


def iota(shape, dim):
    return lax.broadcasted_iota(jnp.int32, shape, dim)


def column(row):
    n = row.shape[1]
    return jnp.sum(
        jnp.where(iota((n, n), 0) == iota((n, n), 1), row.astype(F32), 0.0), axis=1, keepdims=True
    ).astype(jnp.int32)


def as_row(col):
    n = col.shape[0]
    return jnp.sum(
        jnp.where(iota((n, n), 0) == iota((n, n), 1), col.astype(F32), 0.0), axis=0, keepdims=True
    ).astype(jnp.int32)


def hot(index, shape, dim):
    return jnp.where(iota(shape, dim) == index, 1.0, 0.0).astype(BF)


def dot(a, b):
    return jnp.dot(a, b, preferred_element_type=F32)


def dot_t(a, b):
    return lax.dot_general(a, b, (((1,), (1,)), ((), ())), preferred_element_type=F32)


def t_dot(a, b):
    return lax.dot_general(a, b, (((0,), (0,)), ((), ())), preferred_element_type=F32)


def halves(x):
    top = x.astype(BF)
    return top, (x - top.astype(F32)).astype(BF)


def ask_kernel(me_ref, owner_ref, row_ref, asked_ref, pos_ref):
    shards, cap = asked_ref.shape
    heads = owner_ref.shape[1]
    owner = owner_ref[...]
    owner_col = column(owner)
    square = (heads, heads)
    same = owner_col == owner
    slot_row = jnp.sum(
        jnp.where(same & (iota(square, 0) < iota(square, 1)), 1.0, 0.0), axis=0, keepdims=True
    ).astype(jnp.int32)
    slot_col = jnp.sum(
        jnp.where(same & (iota(square, 1) < iota(square, 0)), 1.0, 0.0), axis=1, keepdims=True
    ).astype(jnp.int32)
    pos_ref[...] = owner * cap + slot_row
    value = row_ref[...] + 1
    mine = iota((shards, heads), 0) == owner
    high = jnp.where(mine, (value // 256).astype(F32), 0.0).astype(BF)
    low = jnp.where(mine, (value % 256).astype(F32), 0.0).astype(BF)
    place = hot(slot_col, (heads, cap), 1)
    asked_ref[...] = (256.0 * dot(high, place) + dot(low, place)).astype(jnp.int32) - 1


def take_kernel(row_ref, entity_ref, out_ref):
    count = row_ref.shape[1]
    pick = hot(column(row_ref[...]), (count, entity_ref.shape[0]), 1)
    out_ref[...] = dot(pick, entity_ref[...]).astype(BF)


def wanted_column(wanted_ref):
    return jnp.concatenate(
        [column(wanted_ref[s : s + 1, :]) for s in range(wanted_ref.shape[0])], axis=0
    )


def serve_kernel(wanted_ref, entity_ref, out_ref):
    pick = hot(wanted_column(wanted_ref), (out_ref.shape[0], entity_ref.shape[0]), 1)
    out_ref[...] = dot(pick, entity_ref[...]).astype(BF)


def query_kernel(pos_ref, qrel_ref, fetched_ref, rel_ref, vec_ref, q_ref, prod):
    heads = vec_ref.shape[0]
    rels = rel_ref.shape[0]
    slots = fetched_ref.shape[0]
    vec = dot(hot(column(pos_ref[...]), (heads, slots), 1), fetched_ref[...]).astype(BF)
    vec_ref[...] = vec
    for k in range(rels):
        prod[k] = dot(vec, rel_ref[k])
    for j in range(qrel_ref.shape[0]):
        kind = column(qrel_ref[j : j + 1, :])
        query = prod[0]
        for k in range(1, rels):
            query = jnp.where(kind == k, prod[k], query)
        q_ref[j * heads : (j + 1) * heads, :] = query.astype(BF)


def pair_kernel(q_ref, qrel_ref, tail_ref, ent_ref, *refs):
    blocks, refs = refs[:STOPS], refs[STOPS:]
    weights, (pw_ref, pair_ref, gq) = refs[:STOPS], refs[STOPS:]
    per, heads = qrel_ref.shape
    ents = ent_ref.shape[0]
    for j in range(per):
        here = slice(j * heads, (j + 1) * heads)
        query = q_ref[here, :]
        tail = dot(hot(column(tail_ref[j : j + 1, :]), (heads, ents), 1), ent_ref[...])
        score = jnp.sum(query.astype(F32) * tail, axis=1, keepdims=True)
        pw = jax.nn.sigmoid(score) - 1.0
        pw_ref[j] = pw
        total = pw * tail
        for weight, block in zip(weights, blocks):
            w = (jax.nn.sigmoid(dot_t(query, block[...])) / STOPS).astype(BF)
            weight[here, :] = w
            total = total + dot(w, block[...])
        gq[j] = total
    kinds = [column(qrel_ref[j : j + 1, :]) for j in range(per)]
    for k in range(pair_ref.shape[0]):
        total = jnp.where(kinds[0] == k, gq[0], 0.0)
        for j in range(1, per):
            total = total + jnp.where(kinds[j] == k, gq[j], 0.0)
        pair_ref[k] = total.astype(BF)


def term_kernel(q_ref, weight_ref, term):
    term[...] = t_dot(weight_ref[...], q_ref[...]).astype(term.dtype)


def reversed_bits(value, count):
    return int("0" + format(value, "b").zfill(count)[::-1][:count], 2) if count else 0


def rel_kernel(step, first, outer, me_ref, vec_ref, pair_ref, keep, send, turned, side):
    count, half, width = keep.shape
    inner = 1 - outer
    bits = (width // step // 4).bit_length() - 1
    turned[...] = vec_ref[...].astype(F32).T
    for at in range(width // step):
        flips, line = divmod(at, 1 << bits)
        mask = (flips // 2) << outer | (flips % 2) << inner | reversed_bits(line, bits) << 2
        block = me_ref[0] ^ mask
        side[at * step : (at + 1) * step, :] = turned[
            pl.ds(pl.multiple_of(block * step, step), step), :
        ]
    for k in range(count):
        send[k] = dot(side[half:, :].astype(BF), pair_ref[first + k]).astype(BF)
    for k in range(count):
        keep[k] = dot(side[:half, :].astype(BF), pair_ref[first + k])


def fold_kernel(parts, *refs):
    keeps, gots, refs = refs[:parts], refs[parts : 2 * parts], refs[2 * parts :]
    for n in range(parts):
        count = keeps[n].shape[0]
        rows = slice(n * count, (n + 1) * count)
        total = keeps[n][...] + gots[n][...].astype(F32)
        half = refs[0].shape[1]
        refs[0][rows] = total[:, :half]
        if len(refs) > 1:
            refs[1][rows] = total[:, half:].astype(BF)


def head_kernel(pos_ref, pair_ref, rel_ref, bucket_ref):
    rels, heads, _ = pair_ref.shape
    head = dot_t(pair_ref[0], rel_ref[0])
    for k in range(1, rels):
        head = head + dot_t(pair_ref[k], rel_ref[k])
    slots = bucket_ref.shape[0]
    bucket_ref[...] = dot(hot(pos_ref[...], (slots, heads), 0), head.astype(BF)).astype(BF)


def tail_kernel(tail_ref, q_ref, pw_ref, weight_ref, wanted_ref, out_ref, term, row_ref):
    ents, heads = out_ref.shape[0], tail_ref.shape[1]
    total = jnp.zeros(out_ref.shape, F32)
    for j in range(tail_ref.shape[0]):
        spot = hot(tail_ref[j : j + 1, :], (ents, heads), 0)
        top, rest = halves(pw_ref[j] * q_ref[j * heads : (j + 1) * heads, :].astype(F32))
        total = total + dot(spot, top) + dot(spot, rest)
    out_ref[...] = total
    term[...] = t_dot(weight_ref[...], q_ref[...])
    row_ref[...] = as_row(wanted_column(wanted_ref))


def sum_kernel(reps, me_ref, wanted_ref, neg_ref, returned_ref, base_ref, *refs):
    terms = refs[:STOPS]
    own_ref, outs = refs[STOPS], refs[STOPS + 1 :]
    ents = base_ref.shape[0]
    total = terms[0][...]
    for term in terms[1:]:
        total = total + term[...].astype(F32)
    top, rest = halves(total)
    spot = hot(neg_ref[...], (ents, neg_ref.shape[1]), 0)
    back = hot(wanted_ref[...], (ents, wanted_ref.shape[1]), 0)
    full = base_ref[...] + dot(back, returned_ref[...]) + dot(spot, top) + dot(spot, rest)
    chunk = own_ref.shape[1]
    rep = me_ref[1]
    parts = [full[:, c * chunk : (c + 1) * chunk] for c in range(reps)]

    def pick(number):
        value = parts[0]
        for c in range(1, reps):
            value = jnp.where(number == c, parts[c], value)
        return value

    own_ref[...] = pick(rep)
    for shift, out in enumerate(outs):
        out[...] = pick((rep + shift + 1) % reps).astype(BF)


def kernel(body, outs, scratch=(), smem=0, limit=VMEM):
    def call(*args):
        return pl.pallas_call(
            body,
            out_shape=[o[2](*o[:2]) if len(o) > 2 else jax.ShapeDtypeStruct(*o) for o in outs],
            in_specs=[
                pl.BlockSpec(memory_space=pltpu.SMEM if i < smem else pltpu.VMEM)
                for i in range(len(args))
            ],
            out_specs=[pl.BlockSpec(memory_space=pltpu.VMEM)] * len(outs),
            scratch_shapes=[pltpu.VMEM(s, d) for s, d in scratch],
            compiler_params=pltpu.CompilerParams(vmem_limit_bytes=limit),
        )(*args)

    return call


def far(value):
    return pltpu.with_memory_space_constraint(value, pltpu.HBM)


def per_device(entity, relation, head_owner, head_row, query_rel, tail_row, neg_row):
    shards, reps = lax.axis_size("blk"), lax.axis_size("rep")
    ents, width = entity.shape
    rels = relation.shape[0]
    heads = head_row.shape[0]
    per = query_rel.shape[1]
    rows = neg_row.shape[1]
    cap = max(2, 2 * heads // shards)
    slots = shards * cap
    step = width // shards
    lines = shards // 4
    me = jnp.stack([lax.axis_index("blk"), lax.axis_index("rep")]).astype(jnp.int32)

    def moved(value, distance):
        return lax.ppermute(value, "blk", [((i - distance) % shards, i) for i in range(shards)])

    def flipped(value, bit):
        return lax.ppermute(value, "blk", [(i, i ^ bit) for i in range(shards)])

    def dealt(value, groups=None):
        return lax.all_to_all(
            value, "blk", split_axis=0, concat_axis=0, tiled=True, axis_index_groups=groups
        )

    owner_row = head_owner.reshape(1, heads)
    qrel, tail = query_rel.T, tail_row.T
    (own_block,) = kernel(take_kernel, [((rows, width), BF, HM)], limit=None)(neg_row, entity)
    blocks = [own_block] + [moved(own_block, o) for o in OFFSETS]
    asked, pos = kernel(ask_kernel, [((shards, cap), jnp.int32), ((1, heads), jnp.int32)], limit=None, smem=1)(
        me, owner_row,
        head_row.reshape(1, heads),
    )
    wanted = dealt(asked)
    (served,) = kernel(serve_kernel, [((slots, width), BF, HM)], limit=None)(wanted, entity)
    fetched = dealt(served.reshape(shards, cap, width)).reshape(slots, width)

    many = per * heads
    vec, queries = kernel(
        query_kernel, [((heads, width), BF, VM), ((many, width), BF, VM)], [((rels, heads, width), F32)]
    )(pos, qrel, fetched, relation)
    outs = [((many, rows), BF, HM)] * STOPS + [((per, heads, 1), F32, HM), ((rels, heads, width), BF, VM)]
    *weights, pos_weight, pair = kernel(pair_kernel, outs, [((per, heads, width), F32)])(
        queries, qrel, tail, entity, *blocks
    )

    part = (rels // 2, width // 2, width)

    def relations(first, outer):
        return kernel(
            functools.partial(rel_kernel, step, first, outer),
            [(part, F32, HM), (part, BF, HM)],
            [((width, heads), F32)] * 2,
            smem=1,
        )(me, vec, pair)

    keep_a, send_a = relations(0, 0)
    got_a = flipped(send_a, 1)
    keep_b, send_b = relations(rels // 2, 1)
    got_b = flipped(send_b, 2)
    (buckets,) = kernel(head_kernel, [((slots, width), BF, HM)])(pos, pair, relation)
    returned = dealt(buckets.reshape(shards, cap, width)).reshape(slots, width)
    back = []
    for n, offset in enumerate(OFFSETS):
        (term,) = kernel(term_kernel, [((rows, width), BF, HM)])(queries, weights[n + 1])
        back.append(moved(term, -offset))
    base, own_term, wanted_row = kernel(
        tail_kernel, [((ents, width), F32, HM), ((rows, width), F32, HM), ((1, slots), jnp.int32)]
    )(tail, queries, pos_weight, weights[0], wanted)
    back = [own_term] + back

    def fold(keeps, gots):
        count, size = len(keeps) * keeps[0].shape[0], keeps[0].shape[1]
        outs = [((count, size, width), F32)]
        if size > step:
            outs = [((count, size // 2, width), F32), ((count, size // 2, width), BF, HM)]
        return kernel(functools.partial(fold_kernel, len(keeps)), outs)(*keeps, *gots)

    keep_a, send_a = fold([keep_a], [got_a])
    more_a = flipped(send_a, 2)
    keep_b, send_b = fold([keep_b], [got_b])
    more_b = flipped(send_b, 1)
    keep, *send = fold([keep_a, keep_b], [more_a, more_b])
    for n in range(lines.bit_length() - 1):
        got = flipped(send[0], 4 << n)
        keep, *send = fold([keep], [got])
    grad_rel = keep

    chunk = width // reps
    own, *others = kernel(
        functools.partial(sum_kernel, reps),
        [((ents, chunk), F32)] + [((ents, chunk), BF)] * (reps - 1),
        smem=1,
    )(me, wanted_row, neg_row, *[far(value) for value in (returned, base, *back)])
    grad_entity = own
    for shift, other in enumerate(others):
        route = [(i, (i + shift + 1) % reps) for i in range(reps)]
        grad_entity = grad_entity + lax.ppermute(other, "rep", route).astype(F32)
    return (grad_entity, grad_rel)


def solution(mesh):
    placed = (
        P("blk", None),
        P("rep", None, None),
        P(("blk", "rep"), None),
        P(("blk", "rep")),
        P(("blk", "rep"), None),
        P(("blk", "rep"), None),
        P("blk", "rep"),
    )

    return jax.shard_map(
        per_device,
        mesh=mesh,
        in_specs=placed,
        out_specs=(P("blk", "rep"), P("rep", "blk", None)),
        check_vma=False,
    )
```

```python
import functools

import jax
import jax.numpy as jnp
from jax import lax
from jax.experimental import pallas as pl
from jax.experimental.pallas import tpu as pltpu
from jax.sharding import PartitionSpec as P


STOPS = 6
FORE = STOPS // 2
BACK = STOPS - 1 - FORE
OFFSETS = tuple(range(1, FORE + 1)) + tuple(range(-1, -BACK - 1, -1))
VMEM, WIDE = 12 << 20, 16 << 20
BF = jnp.bfloat16
F32 = jnp.float32
VM, HM = pltpu.VMEM, pltpu.HBM


def iota(shape, dim):
    return lax.broadcasted_iota(jnp.int32, shape, dim)


def column(row):
    n = row.shape[1]
    return jnp.sum(
        jnp.where(iota((n, n), 0) == iota((n, n), 1), row.astype(F32), 0.0), axis=1, keepdims=True
    ).astype(jnp.int32)


def as_row(col):
    n = col.shape[0]
    return jnp.sum(
        jnp.where(iota((n, n), 0) == iota((n, n), 1), col.astype(F32), 0.0), axis=0, keepdims=True
    ).astype(jnp.int32)


def hot(index, shape, dim):
    return jnp.where(iota(shape, dim) == index, 1.0, 0.0).astype(BF)


def dot(a, b):
    return jnp.dot(a, b, preferred_element_type=F32)


def dot_t(a, b):
    return lax.dot_general(a, b, (((1,), (1,)), ((), ())), preferred_element_type=F32)


def t_dot(a, b):
    return lax.dot_general(a, b, (((0,), (0,)), ((), ())), preferred_element_type=F32)


def halves(x):
    top = x.astype(BF)
    return top, (x - top.astype(F32)).astype(BF)


def ask_kernel(me_ref, owner_ref, row_ref, asked_ref, pos_ref):
    shards, cap = asked_ref.shape
    heads = owner_ref.shape[1]
    owner = owner_ref[...]
    owner_col = column(owner)
    square = (heads, heads)
    same = owner_col == owner
    slot_row = jnp.sum(
        jnp.where(same & (iota(square, 0) < iota(square, 1)), 1.0, 0.0), axis=0, keepdims=True
    ).astype(jnp.int32)
    slot_col = jnp.sum(
        jnp.where(same & (iota(square, 1) < iota(square, 0)), 1.0, 0.0), axis=1, keepdims=True
    ).astype(jnp.int32)
    pos_ref[...] = owner * cap + slot_row
    value = row_ref[...] + 1
    mine = iota((shards, heads), 0) == owner
    high = jnp.where(mine, (value // 256).astype(F32), 0.0).astype(BF)
    low = jnp.where(mine, (value % 256).astype(F32), 0.0).astype(BF)
    place = hot(slot_col, (heads, cap), 1)
    asked_ref[...] = (256.0 * dot(high, place) + dot(low, place)).astype(jnp.int32) - 1


def take_kernel(row_ref, entity_ref, out_ref):
    count = row_ref.shape[1]
    pick = hot(column(row_ref[...]), (count, entity_ref.shape[0]), 1)
    out_ref[...] = dot(pick, entity_ref[...]).astype(BF)


def wanted_column(wanted_ref):
    return jnp.concatenate(
        [column(wanted_ref[s : s + 1, :]) for s in range(wanted_ref.shape[0])], axis=0
    )


def serve_kernel(wanted_ref, entity_ref, out_ref):
    pick = hot(wanted_column(wanted_ref), (out_ref.shape[0], entity_ref.shape[0]), 1)
    out_ref[...] = dot(pick, entity_ref[...]).astype(BF)


def query_kernel(pos_ref, qrel_ref, fetched_ref, rel_ref, turned, q_ref, prod):
    rels, _ = rel_ref.shape[:2]
    heads = qrel_ref.shape[1]
    vec = dot(hot(column(pos_ref[...]), (heads, fetched_ref.shape[0]), 1), fetched_ref[...]).astype(BF)
    for k in range(rels):
        prod[k] = dot(vec, rel_ref[k])
    turned[...] = vec.astype(F32).T
    for j in range(qrel_ref.shape[0]):
        kind = column(qrel_ref[j : j + 1, :])
        query = prod[0]
        for k in range(1, rels):
            query = jnp.where(kind == k, prod[k], query)
        q_ref[j * heads : (j + 1) * heads, :] = query.astype(BF)


def reversed_bits(value, count):
    return int("0" + format(value, "b").zfill(count)[::-1][:count], 2) if count else 0


def arrange(step, outer, upper, me, turned, side):
    width = turned.shape[0]
    bits = (width // step // 4).bit_length() - 1
    for at in range(width // step // 2):
        flip, line = divmod(at, 1 << bits)
        mask = upper << outer | flip << (1 - outer) | reversed_bits(line, bits) << 2
        side[at * step : (at + 1) * step, :] = turned[
            pl.ds(pl.multiple_of((me ^ mask) * step, step), step), :
        ]


def visit_kernel(step, me_ref, turned, q_ref, qrel_ref, tail_ref, ent_ref, *refs):
    blocks, refs = refs[:STOPS], refs[STOPS:]
    pw_ref, pair_ref, *sends = refs[:4]
    weights, refs = refs[4 : 4 + STOPS], refs[4 + STOPS :]
    near, weight, gq, side, load_sems, store_sems = refs
    per, heads = qrel_ref.shape
    rels = pair_ref.shape[0]
    rows = blocks[0].shape[0]
    loads = [
        pltpu.make_async_copy(block, near.at[n * rows : (n + 1) * rows], load_sems.at[n])
        for n, block in enumerate(blocks)
    ]
    for load in loads:
        load.start()
    kinds = [column(qrel_ref[j : j + 1, :]) for j in range(per)]
    for j in range(per):
        here = slice(j * heads, (j + 1) * heads)
        query = q_ref[here, :]
        tail = dot(hot(column(tail_ref[j : j + 1, :]), (heads, ent_ref.shape[0]), 1), ent_ref[...])
        score = jnp.sum(query.astype(F32) * tail, axis=1, keepdims=True)
        pw = jax.nn.sigmoid(score) - 1.0
        pw_ref[j] = pw
        gq[j] = pw * tail
    for load in loads:
        load.wait()
    stores = []
    for j in range(per):
        here = slice(j * heads, (j + 1) * heads)
        weight[here, :] = (jax.nn.sigmoid(dot_t(q_ref[here, :], near[...])) / STOPS).astype(BF)
        gq[j] = gq[j] + dot(weight[here, :], near[...])
        for n, out in enumerate(weights):
            stores.append(
                pltpu.make_async_copy(
                    weight.at[here, n * rows : (n + 1) * rows], out.at[here], store_sems.at[n, j]
                )
            )
            stores[-1].start()
    for k in range(rels):
        total = jnp.where(kinds[0] == k, gq[0], 0.0)
        for j in range(1, per):
            total = total + jnp.where(kinds[j] == k, gq[j], 0.0)
        pair_ref[k] = total.astype(BF)
    for outer, send in enumerate(sends):
        arrange(step, outer, 1, me_ref[0], turned, side)
        for k in range(send.shape[0]):
            send[k] = dot(side[...].astype(BF), pair_ref[outer * send.shape[0] + k]).astype(BF)
    for store in stores:
        store.wait()


def term_kernel(q_ref, weight_ref, term):
    term[...] = t_dot(weight_ref[...], q_ref[...]).astype(term.dtype)


def keep_kernel(step, me_ref, turned, pair_ref, keep_a, keep_b, side):
    for outer, keep in enumerate((keep_a, keep_b)):
        arrange(step, outer, 0, me_ref[0], turned, side)
        for k in range(keep.shape[0]):
            keep[k] = dot(side[...].astype(BF), pair_ref[outer * keep.shape[0] + k])


def fold_kernel(parts, *refs):
    keeps, gots, refs = refs[:parts], refs[parts : 2 * parts], refs[2 * parts :]
    for n in range(parts):
        count = keeps[n].shape[0]
        rows = slice(n * count, (n + 1) * count)
        total = keeps[n][...] + gots[n][...].astype(F32)
        half = refs[0].shape[1]
        refs[0][rows] = total[:, :half]
        if len(refs) > 1:
            refs[1][rows] = total[:, half:].astype(BF)


def head_kernel(pos_ref, pair_ref, rel_ref, bucket_ref):
    rels, heads, _ = pair_ref.shape
    head = dot_t(pair_ref[0], rel_ref[0])
    for k in range(1, rels):
        head = head + dot_t(pair_ref[k], rel_ref[k])
    slots = bucket_ref.shape[0]
    bucket_ref[...] = dot(hot(pos_ref[...], (slots, heads), 0), head.astype(BF)).astype(BF)


def tail_kernel(tail_ref, q_ref, pw_ref, weight_ref, wanted_ref, out_ref, term, row_ref):
    ents, heads = out_ref.shape[0], tail_ref.shape[1]
    total = jnp.zeros(out_ref.shape, F32)
    for j in range(tail_ref.shape[0]):
        spot = hot(tail_ref[j : j + 1, :], (ents, heads), 0)
        top, rest = halves(pw_ref[j] * q_ref[j * heads : (j + 1) * heads, :].astype(F32))
        total = total + dot(spot, top) + dot(spot, rest)
    out_ref[...] = total
    term[...] = t_dot(weight_ref[...], q_ref[...])
    row_ref[...] = as_row(wanted_column(wanted_ref))


def sum_kernel(reps, me_ref, wanted_ref, neg_ref, returned_ref, base_ref, *refs):
    terms = refs[:STOPS]
    own_ref, outs = refs[STOPS], refs[STOPS + 1 :]
    ents = base_ref.shape[0]
    total = terms[0][...]
    for term in terms[1:]:
        total = total + term[...].astype(F32)
    top, rest = halves(total)
    spot = hot(neg_ref[...], (ents, neg_ref.shape[1]), 0)
    back = hot(wanted_ref[...], (ents, wanted_ref.shape[1]), 0)
    full = base_ref[...] + dot(back, returned_ref[...]) + dot(spot, top) + dot(spot, rest)
    chunk = own_ref.shape[1]
    rep = me_ref[1]
    parts = [full[:, c * chunk : (c + 1) * chunk] for c in range(reps)]

    def pick(number):
        value = parts[0]
        for c in range(1, reps):
            value = jnp.where(number == c, parts[c], value)
        return value

    own_ref[...] = pick(rep)
    for shift, out in enumerate(outs):
        out[...] = pick((rep + shift + 1) % reps).astype(BF)


def kernel(body, outs, scratch=(), smem=0, limit=VMEM, wild=0, wild_outs=0):
    def call(*args):
        count = len(args)

        def place(i):
            if i < smem:
                return pltpu.SMEM
            return pl.ANY if i >= count - wild else pltpu.VMEM

        return pl.pallas_call(
            body,
            out_shape=[o[2](*o[:2]) if len(o) > 2 else jax.ShapeDtypeStruct(*o) for o in outs],
            in_specs=[pl.BlockSpec(memory_space=place(i)) for i in range(count)],
            out_specs=[
                pl.BlockSpec(memory_space=pl.ANY if i >= len(outs) - wild_outs else pltpu.VMEM)
                for i in range(len(outs))
            ],
            scratch_shapes=[pltpu.VMEM(*s) if isinstance(s, tuple) else s for s in scratch],
            compiler_params=pltpu.CompilerParams(vmem_limit_bytes=limit),
        )(*args)

    return call


def far(value):
    return pltpu.with_memory_space_constraint(value, pltpu.HBM)


def per_device(entity, relation, head_owner, head_row, query_rel, tail_row, neg_row):
    shards, reps = lax.axis_size("blk"), lax.axis_size("rep")
    ents, width = entity.shape
    rels = relation.shape[0]
    heads = head_row.shape[0]
    per = query_rel.shape[1]
    rows = neg_row.shape[1]
    cap = max(2, 2 * heads // shards)
    slots = shards * cap
    step = width // shards
    lines = shards // 4
    me = jnp.stack([lax.axis_index("blk"), lax.axis_index("rep")]).astype(jnp.int32)

    def moved(value, distance):
        return lax.ppermute(value, "blk", [((i - distance) % shards, i) for i in range(shards)])

    def flipped(value, bit):
        return lax.ppermute(value, "blk", [(i, i ^ bit) for i in range(shards)])

    def dealt(value, groups=None):
        return lax.all_to_all(
            value, "blk", split_axis=0, concat_axis=0, tiled=True, axis_index_groups=groups
        )

    owner_row = head_owner.reshape(1, heads)
    qrel, tail = query_rel.T, tail_row.T
    (own_block,) = kernel(take_kernel, [((rows, width), BF, HM)], limit=None)(neg_row, entity)
    blocks = [own_block] + [moved(own_block, o) for o in OFFSETS]
    asked, pos = kernel(ask_kernel, [((shards, cap), jnp.int32), ((1, heads), jnp.int32)], limit=None, smem=1)(
        me, owner_row,
        head_row.reshape(1, heads),
    )
    wanted = dealt(asked)
    (served,) = kernel(serve_kernel, [((slots, width), BF, HM)], limit=None)(wanted, entity)
    fetched = dealt(served.reshape(shards, cap, width)).reshape(slots, width)

    many = per * heads
    turned, queries = kernel(
        query_kernel,
        [((width, heads), F32, VM), ((many, width), BF, VM)],
        [((rels, heads, width), F32)],
    )(pos, qrel, fetched, relation)
    part = (rels // 2, width // 2, width)
    side = ((width // 2, heads), F32)
    pos_weight, pair, send_a, send_b, *weights = kernel(
        functools.partial(visit_kernel, step),
        [((per, heads, 1), F32, HM), ((rels, heads, width), BF, VM)]
        + [(part, BF, HM)] * 2
        + [((many, rows), BF, HM)] * STOPS,
        [
            ((STOPS * rows, width), BF),
            ((many, STOPS * rows), BF),
            ((per, heads, width), F32),
            side,
            pltpu.SemaphoreType.DMA((STOPS,)),
            pltpu.SemaphoreType.DMA((STOPS, per)),
        ],
        smem=1,
        wild=STOPS,
        wild_outs=STOPS,
        limit=WIDE,
    )(me, turned, queries, qrel, tail, entity, *[far(block) for block in blocks])

    got_a = flipped(send_a, 1)
    got_b = flipped(send_b, 2)
    keep_a, keep_b = kernel(functools.partial(keep_kernel, step), [(part, F32, HM)] * 2, [side], smem=1)(
        me, turned, pair,
    )
    (buckets,) = kernel(head_kernel, [((slots, width), BF, HM)])(pos, pair, relation)
    returned = dealt(buckets.reshape(shards, cap, width)).reshape(slots, width)
    back = []
    for n, offset in enumerate(OFFSETS):
        (term,) = kernel(term_kernel, [((rows, width), BF, HM)])(queries, weights[n + 1])
        back.append(moved(term, -offset))
    base, own_term, wanted_row = kernel(
        tail_kernel, [((ents, width), F32, HM), ((rows, width), F32, HM), ((1, slots), jnp.int32)]
    )(tail, queries, pos_weight, weights[0], wanted)
    back = [own_term] + back

    def fold(keeps, gots):
        count, size = len(keeps) * keeps[0].shape[0], keeps[0].shape[1]
        outs = [((count, size, width), F32)]
        if size > step:
            outs = [((count, size // 2, width), F32), ((count, size // 2, width), BF, HM)]
        return kernel(functools.partial(fold_kernel, len(keeps)), outs)(*keeps, *gots)

    keep_a, send_a = fold([keep_a], [got_a])
    more_a = flipped(send_a, 2)
    keep_b, send_b = fold([keep_b], [got_b])
    more_b = flipped(send_b, 1)
    keep, *send = fold([keep_a, keep_b], [more_a, more_b])
    for n in range(lines.bit_length() - 1):
        got = flipped(send[0], 4 << n)
        keep, *send = fold([keep], [got])
    grad_rel = keep

    chunk = width // reps
    own, *others = kernel(
        functools.partial(sum_kernel, reps),
        [((ents, chunk), F32)] + [((ents, chunk), BF)] * (reps - 1),
        smem=1,
    )(me, wanted_row, neg_row, *[far(value) for value in (returned, base, *back)])
    grad_entity = own
    for shift, other in enumerate(others):
        route = [(i, (i + shift + 1) % reps) for i in range(reps)]
        grad_entity = grad_entity + lax.ppermute(other, "rep", route).astype(F32)
    return (grad_entity, grad_rel)


def solution(mesh):
    placed = (
        P("blk", None),
        P("rep", None, None),
        P(("blk", "rep"), None),
        P(("blk", "rep")),
        P(("blk", "rep"), None),
        P(("blk", "rep"), None),
        P("blk", "rep"),
    )

    return jax.shard_map(
        per_device,
        mesh=mesh,
        in_specs=placed,
        out_specs=(P("blk", "rep"), P("rep", "blk", None)),
        check_vma=False,
    )
```

```python
import functools

import jax
import jax.numpy as jnp
from jax import lax
from jax.experimental import pallas as pl
from jax.experimental.pallas import tpu as pltpu
from jax.sharding import PartitionSpec as P


STOPS = 6
FORE = STOPS // 2
BACK = STOPS - 1 - FORE
OFFSETS = tuple(range(1, FORE + 1)) + tuple(range(-1, -BACK - 1, -1))
VMEM, WIDE = 12 << 20, 16 << 20
BF = jnp.bfloat16
F32 = jnp.float32
VM, HM = pltpu.VMEM, pltpu.HBM


def iota(shape, dim):
    return lax.broadcasted_iota(jnp.int32, shape, dim)


def column(row):
    n = row.shape[1]
    return jnp.sum(
        jnp.where(iota((n, n), 0) == iota((n, n), 1), row.astype(F32), 0.0), axis=1, keepdims=True
    ).astype(jnp.int32)


def as_row(col):
    n = col.shape[0]
    return jnp.sum(
        jnp.where(iota((n, n), 0) == iota((n, n), 1), col.astype(F32), 0.0), axis=0, keepdims=True
    ).astype(jnp.int32)


def hot(index, shape, dim):
    return jnp.where(iota(shape, dim) == index, 1.0, 0.0).astype(BF)


def dot(a, b):
    return jnp.dot(a, b, preferred_element_type=F32)


def dot_t(a, b):
    return lax.dot_general(a, b, (((1,), (1,)), ((), ())), preferred_element_type=F32)


def t_dot(a, b):
    return lax.dot_general(a, b, (((0,), (0,)), ((), ())), preferred_element_type=F32)


def halves(x):
    top = x.astype(BF)
    return top, (x - top.astype(F32)).astype(BF)


def ask_kernel(me_ref, owner_ref, row_ref, asked_ref, pos_ref):
    shards, cap = asked_ref.shape
    heads = owner_ref.shape[1]
    owner = owner_ref[...]
    owner_col = column(owner)
    square = (heads, heads)
    same = owner_col == owner
    slot_row = jnp.sum(
        jnp.where(same & (iota(square, 0) < iota(square, 1)), 1.0, 0.0), axis=0, keepdims=True
    ).astype(jnp.int32)
    slot_col = jnp.sum(
        jnp.where(same & (iota(square, 1) < iota(square, 0)), 1.0, 0.0), axis=1, keepdims=True
    ).astype(jnp.int32)
    pos_ref[...] = owner * cap + slot_row
    value = row_ref[...] + 1
    mine = iota((shards, heads), 0) == owner
    high = jnp.where(mine, (value // 256).astype(F32), 0.0).astype(BF)
    low = jnp.where(mine, (value % 256).astype(F32), 0.0).astype(BF)
    place = hot(slot_col, (heads, cap), 1)
    asked_ref[...] = (256.0 * dot(high, place) + dot(low, place)).astype(jnp.int32) - 1


def take_kernel(row_ref, entity_ref, out_ref):
    count = row_ref.shape[1]
    pick = hot(column(row_ref[...]), (count, entity_ref.shape[0]), 1)
    out_ref[...] = dot(pick, entity_ref[...]).astype(BF)


def wanted_column(wanted_ref):
    return jnp.concatenate(
        [column(wanted_ref[s : s + 1, :]) for s in range(wanted_ref.shape[0])], axis=0
    )


def serve_kernel(wanted_ref, entity_ref, out_ref, table, sem):
    load = pltpu.make_async_copy(entity_ref, table, sem.at[0])
    load.start()
    pick = hot(wanted_column(wanted_ref), (out_ref.shape[0], table.shape[0]), 1)
    load.wait()
    out_ref[...] = dot(pick, table[...]).astype(BF)


def query_kernel(pos_ref, qrel_ref, fetched_ref, rel_ref, turned, q_ref, prod):
    rels, _ = rel_ref.shape[:2]
    heads = qrel_ref.shape[1]
    vec = dot(hot(column(pos_ref[...]), (heads, fetched_ref.shape[0]), 1), fetched_ref[...]).astype(BF)
    for k in range(rels):
        prod[k] = dot(vec, rel_ref[k])
    turned[...] = vec.astype(F32).T
    for j in range(qrel_ref.shape[0]):
        kind = column(qrel_ref[j : j + 1, :])
        query = prod[0]
        for k in range(1, rels):
            query = jnp.where(kind == k, prod[k], query)
        q_ref[j * heads : (j + 1) * heads, :] = query.astype(BF)


def reversed_bits(value, count):
    return int("0" + format(value, "b").zfill(count)[::-1][:count], 2) if count else 0


def arrange(step, outer, upper, me, turned, side):
    width = turned.shape[0]
    bits = (width // step // 4).bit_length() - 1
    for at in range(width // step // 2):
        flip, line = divmod(at, 1 << bits)
        mask = upper << outer | flip << (1 - outer) | reversed_bits(line, bits) << 2
        side[at * step : (at + 1) * step, :] = turned[
            pl.ds(pl.multiple_of((me ^ mask) * step, step), step), :
        ]


def visit_kernel(step, me_ref, turned, q_ref, qrel_ref, tail_ref, ent_ref, *refs):
    blocks, refs = refs[:STOPS], refs[STOPS:]
    pw_ref, pair_ref, *sends = refs[:4]
    weights, refs = refs[4 : 4 + STOPS], refs[4 + STOPS :]
    near, weight, gq, side, load_sems, store_sems = refs
    per, heads = qrel_ref.shape
    rels = pair_ref.shape[0]
    rows = blocks[0].shape[0]
    loads = [
        pltpu.make_async_copy(block, near.at[n * rows : (n + 1) * rows], load_sems.at[n])
        for n, block in enumerate(blocks)
    ]
    for load in loads:
        load.start()
    kinds = [column(qrel_ref[j : j + 1, :]) for j in range(per)]
    for j in range(per):
        here = slice(j * heads, (j + 1) * heads)
        query = q_ref[here, :]
        tail = dot(hot(column(tail_ref[j : j + 1, :]), (heads, ent_ref.shape[0]), 1), ent_ref[...])
        score = jnp.sum(query.astype(F32) * tail, axis=1, keepdims=True)
        pw = jax.nn.sigmoid(score) - 1.0
        pw_ref[j] = pw
        gq[j] = pw * tail
    for load in loads:
        load.wait()
    stores = []
    for j in range(per):
        here = slice(j * heads, (j + 1) * heads)
        weight[here, :] = (jax.nn.sigmoid(dot_t(q_ref[here, :], near[...])) / STOPS).astype(BF)
        gq[j] = gq[j] + dot(weight[here, :], near[...])
        for n, out in enumerate(weights):
            stores.append(
                pltpu.make_async_copy(
                    weight.at[here, n * rows : (n + 1) * rows], out.at[here], store_sems.at[n, j]
                )
            )
            stores[-1].start()
    for k in range(rels):
        total = jnp.where(kinds[0] == k, gq[0], 0.0)
        for j in range(1, per):
            total = total + jnp.where(kinds[j] == k, gq[j], 0.0)
        pair_ref[k] = total.astype(BF)
    for outer, send in enumerate(sends):
        arrange(step, outer, 1, me_ref[0], turned, side)
        for k in range(send.shape[0]):
            send[k] = dot(side[...].astype(BF), pair_ref[outer * send.shape[0] + k]).astype(BF)
    for store in stores:
        store.wait()


def term_kernel(q_ref, weight_ref, term):
    term[...] = t_dot(weight_ref[...], q_ref[...]).astype(term.dtype)


def fold_kernel(parts, *refs):
    keeps, gots, refs = refs[:parts], refs[parts : 2 * parts], refs[2 * parts :]
    for n in range(parts):
        count = keeps[n].shape[0]
        rows = slice(n * count, (n + 1) * count)
        total = keeps[n][...] + gots[n][...].astype(F32)
        half = refs[0].shape[1]
        refs[0][rows] = total[:, :half]
        if len(refs) > 1:
            refs[1][rows] = total[:, half:].astype(BF)


def head_kernel(step, me_ref, pos_ref, pair_ref, rel_ref, turned, bucket_ref, keep_a, keep_b, side):
    rels, heads, _ = pair_ref.shape
    head = dot_t(pair_ref[0], rel_ref[0])
    for k in range(1, rels):
        head = head + dot_t(pair_ref[k], rel_ref[k])
    slots = bucket_ref.shape[0]
    bucket_ref[...] = dot(hot(pos_ref[...], (slots, heads), 0), head.astype(BF)).astype(BF)
    for outer, keep in enumerate((keep_a, keep_b)):
        arrange(step, outer, 0, me_ref[0], turned, side)
        for k in range(keep.shape[0]):
            keep[k] = dot(side[...].astype(BF), pair_ref[outer * keep.shape[0] + k])


def tail_kernel(tail_ref, q_ref, pw_ref, weight_ref, wanted_ref, out_ref, term, row_ref):
    ents, heads = out_ref.shape[0], tail_ref.shape[1]
    total = jnp.zeros(out_ref.shape, F32)
    for j in range(tail_ref.shape[0]):
        spot = hot(tail_ref[j : j + 1, :], (ents, heads), 0)
        top, rest = halves(pw_ref[j] * q_ref[j * heads : (j + 1) * heads, :].astype(F32))
        total = total + dot(spot, top) + dot(spot, rest)
    out_ref[...] = total
    term[...] = t_dot(weight_ref[...], q_ref[...])
    row_ref[...] = as_row(wanted_column(wanted_ref))


def sum_kernel(reps, me_ref, wanted_ref, neg_ref, returned_ref, base_ref, *refs):
    terms = refs[:STOPS]
    own_ref, outs = refs[STOPS], refs[STOPS + 1 :]
    ents = base_ref.shape[0]
    total = terms[0][...]
    for term in terms[1:]:
        total = total + term[...].astype(F32)
    top, rest = halves(total)
    spot = hot(neg_ref[...], (ents, neg_ref.shape[1]), 0)
    back = hot(wanted_ref[...], (ents, wanted_ref.shape[1]), 0)
    full = base_ref[...] + dot(back, returned_ref[...]) + dot(spot, top) + dot(spot, rest)
    chunk = own_ref.shape[1]
    rep = me_ref[1]
    parts = [full[:, c * chunk : (c + 1) * chunk] for c in range(reps)]

    def pick(number):
        value = parts[0]
        for c in range(1, reps):
            value = jnp.where(number == c, parts[c], value)
        return value

    own_ref[...] = pick(rep)
    for shift, out in enumerate(outs):
        out[...] = pick((rep + shift + 1) % reps).astype(BF)


def kernel(body, outs, scratch=(), smem=0, limit=VMEM, wild=0, wild_outs=0):
    def call(*args):
        count = len(args)

        def place(i):
            if i < smem:
                return pltpu.SMEM
            return pl.ANY if i >= count - wild else pltpu.VMEM

        return pl.pallas_call(
            body,
            out_shape=[o[2](*o[:2]) if len(o) > 2 else jax.ShapeDtypeStruct(*o) for o in outs],
            in_specs=[pl.BlockSpec(memory_space=place(i)) for i in range(count)],
            out_specs=[
                pl.BlockSpec(memory_space=pl.ANY if i >= len(outs) - wild_outs else pltpu.VMEM)
                for i in range(len(outs))
            ],
            scratch_shapes=[pltpu.VMEM(*s) if isinstance(s, tuple) else s for s in scratch],
            compiler_params=pltpu.CompilerParams(vmem_limit_bytes=limit),
        )(*args)

    return call


def far(value):
    return pltpu.with_memory_space_constraint(value, pltpu.HBM)


def per_device(entity, relation, head_owner, head_row, query_rel, tail_row, neg_row):
    shards, reps = lax.axis_size("blk"), lax.axis_size("rep")
    ents, width = entity.shape
    rels = relation.shape[0]
    heads = head_row.shape[0]
    per = query_rel.shape[1]
    rows = neg_row.shape[1]
    cap = max(2, 2 * heads // shards)
    slots = shards * cap
    step = width // shards
    lines = shards // 4
    me = jnp.stack([lax.axis_index("blk"), lax.axis_index("rep")]).astype(jnp.int32)

    def moved(value, distance):
        return lax.ppermute(value, "blk", [((i - distance) % shards, i) for i in range(shards)])

    def flipped(value, bit):
        return lax.ppermute(value, "blk", [(i, i ^ bit) for i in range(shards)])

    def dealt(value, groups=None):
        return lax.all_to_all(
            value, "blk", split_axis=0, concat_axis=0, tiled=True, axis_index_groups=groups
        )

    owner_row = head_owner.reshape(1, heads)
    qrel, tail = query_rel.T, tail_row.T
    (own_block,) = kernel(take_kernel, [((rows, width), BF, HM)], limit=None)(neg_row, entity)
    blocks = [own_block] + [moved(own_block, o) for o in OFFSETS]
    asked, pos = kernel(ask_kernel, [((shards, cap), jnp.int32), ((1, heads), jnp.int32)], limit=None, smem=1)(
        me, owner_row,
        head_row.reshape(1, heads),
    )
    wanted = dealt(asked)
    (served,) = kernel(
        serve_kernel,
        [((slots, width), BF, HM)],
        [((ents, width), BF), pltpu.SemaphoreType.DMA((1,))],
        wild=1,
    )(wanted, far(entity))
    fetched = dealt(served.reshape(shards, cap, width)).reshape(slots, width)

    many = per * heads
    turned, queries = kernel(
        query_kernel,
        [((width, heads), F32, VM), ((many, width), BF, VM)],
        [((rels, heads, width), F32)],
    )(pos, qrel, fetched, relation)
    part = (rels // 2, width // 2, width)
    side = ((width // 2, heads), F32)
    pos_weight, pair, send_a, send_b, *weights = kernel(
        functools.partial(visit_kernel, step),
        [((per, heads, 1), F32, HM), ((rels, heads, width), BF, VM)]
        + [(part, BF, HM)] * 2
        + [((many, rows), BF, HM)] * STOPS,
        [
            ((STOPS * rows, width), BF),
            ((many, STOPS * rows), BF),
            ((per, heads, width), F32),
            side,
            pltpu.SemaphoreType.DMA((STOPS,)),
            pltpu.SemaphoreType.DMA((STOPS, per)),
        ],
        smem=1,
        wild=STOPS,
        wild_outs=STOPS,
        limit=WIDE,
    )(me, turned, queries, qrel, tail, entity, *[far(block) for block in blocks])

    got_a = flipped(send_a, 1)
    got_b = flipped(send_b, 2)
    buckets, keep_a, keep_b = kernel(
        functools.partial(head_kernel, step),
        [((slots, width), BF, HM), (part, F32, HM), (part, F32, HM)],
        [side],
        smem=1,
    )(me, pos, pair, relation, turned)
    returned = dealt(buckets.reshape(shards, cap, width)).reshape(slots, width)
    back = []
    for n, offset in enumerate(OFFSETS):
        (term,) = kernel(term_kernel, [((rows, width), BF, HM)])(queries, weights[n + 1])
        back.append(moved(term, -offset))
    base, own_term, wanted_row = kernel(
        tail_kernel, [((ents, width), F32, HM), ((rows, width), F32, HM), ((1, slots), jnp.int32)]
    )(tail, queries, pos_weight, weights[0], wanted)
    back = [own_term] + back

    def fold(keeps, gots):
        count, size = len(keeps) * keeps[0].shape[0], keeps[0].shape[1]
        outs = [((count, size, width), F32)]
        if size > step:
            outs = [((count, size // 2, width), F32), ((count, size // 2, width), BF, HM)]
        return kernel(functools.partial(fold_kernel, len(keeps)), outs)(*keeps, *gots)

    keep_a, send_a = fold([keep_a], [got_a])
    more_a = flipped(send_a, 2)
    keep_b, send_b = fold([keep_b], [got_b])
    more_b = flipped(send_b, 1)
    keep, *send = fold([keep_a, keep_b], [more_a, more_b])
    for n in range(lines.bit_length() - 1):
        got = flipped(send[0], 4 << n)
        keep, *send = fold([keep], [got])
    grad_rel = keep

    chunk = width // reps
    own, *others = kernel(
        functools.partial(sum_kernel, reps),
        [((ents, chunk), F32)] + [((ents, chunk), BF)] * (reps - 1),
        smem=1,
    )(me, wanted_row, neg_row, *[far(value) for value in (returned, base, *back)])
    grad_entity = own
    for shift, other in enumerate(others):
        route = [(i, (i + shift + 1) % reps) for i in range(reps)]
        grad_entity = grad_entity + lax.ppermute(other, "rep", route).astype(F32)
    return (grad_entity, grad_rel)


def solution(mesh):
    placed = (
        P("blk", None),
        P("rep", None, None),
        P(("blk", "rep"), None),
        P(("blk", "rep")),
        P(("blk", "rep"), None),
        P(("blk", "rep"), None),
        P("blk", "rep"),
    )

    return jax.shard_map(
        per_device,
        mesh=mesh,
        in_specs=placed,
        out_specs=(P("blk", "rep"), P("rep", "blk", None)),
        check_vma=False,
    )
```

```python
import functools

import jax
import jax.numpy as jnp
from jax import lax
from jax.experimental import pallas as pl
from jax.experimental.pallas import tpu as pltpu
from jax.sharding import PartitionSpec as P


STOPS = 6
FORE = STOPS // 2
BACK = STOPS - 1 - FORE
OFFSETS = tuple(range(1, FORE + 1)) + tuple(range(-1, -BACK - 1, -1))
VMEM, WIDE = 12 << 20, 16 << 20
BF = jnp.bfloat16
F32 = jnp.float32
VM, HM = pltpu.VMEM, pltpu.HBM


def iota(shape, dim):
    return lax.broadcasted_iota(jnp.int32, shape, dim)


def column(row):
    n = row.shape[1]
    return jnp.sum(
        jnp.where(iota((n, n), 0) == iota((n, n), 1), row.astype(F32), 0.0), axis=1, keepdims=True
    ).astype(jnp.int32)


def as_row(col):
    n = col.shape[0]
    return jnp.sum(
        jnp.where(iota((n, n), 0) == iota((n, n), 1), col.astype(F32), 0.0), axis=0, keepdims=True
    ).astype(jnp.int32)


def hot(index, shape, dim):
    return jnp.where(iota(shape, dim) == index, 1.0, 0.0).astype(BF)


def dot(a, b):
    return jnp.dot(a, b, preferred_element_type=F32)


def dot_t(a, b):
    return lax.dot_general(a, b, (((1,), (1,)), ((), ())), preferred_element_type=F32)


def t_dot(a, b):
    return lax.dot_general(a, b, (((0,), (0,)), ((), ())), preferred_element_type=F32)


def halves(x):
    top = x.astype(BF)
    return top, (x - top.astype(F32)).astype(BF)


def ask_kernel(me_ref, owner_ref, row_ref, asked_ref, pos_ref):
    shards, cap = asked_ref.shape
    heads = owner_ref.shape[1]
    owner = owner_ref[...]
    owner_col = column(owner)
    square = (heads, heads)
    same = owner_col == owner
    slot_row = jnp.sum(
        jnp.where(same & (iota(square, 0) < iota(square, 1)), 1.0, 0.0), axis=0, keepdims=True
    ).astype(jnp.int32)
    slot_col = jnp.sum(
        jnp.where(same & (iota(square, 1) < iota(square, 0)), 1.0, 0.0), axis=1, keepdims=True
    ).astype(jnp.int32)
    pos_ref[...] = owner * cap + slot_row
    value = row_ref[...] + 1
    mine = iota((shards, heads), 0) == owner
    high = jnp.where(mine, (value // 256).astype(F32), 0.0).astype(BF)
    low = jnp.where(mine, (value % 256).astype(F32), 0.0).astype(BF)
    place = hot(slot_col, (heads, cap), 1)
    asked_ref[...] = (256.0 * dot(high, place) + dot(low, place)).astype(jnp.int32) - 1


def take_kernel(row_ref, entity_ref, out_ref):
    count = row_ref.shape[1]
    pick = hot(column(row_ref[...]), (count, entity_ref.shape[0]), 1)
    out_ref[...] = dot(pick, entity_ref[...]).astype(BF)


def wanted_column(wanted_ref):
    return jnp.concatenate(
        [column(wanted_ref[s : s + 1, :]) for s in range(wanted_ref.shape[0])], axis=0
    )


def serve_kernel(wanted_ref, entity_ref, out_ref, table, sem):
    load = pltpu.make_async_copy(entity_ref, table, sem.at[0])
    load.start()
    pick = hot(wanted_column(wanted_ref), (out_ref.shape[0], table.shape[0]), 1)
    load.wait()
    out_ref[...] = dot(pick, table[...]).astype(BF)


def query_kernel(pos_ref, qrel_ref, fetched_ref, rel_ref, turned, q_ref, prod):
    rels, _ = rel_ref.shape[:2]
    heads = qrel_ref.shape[1]
    vec = dot(hot(column(pos_ref[...]), (heads, fetched_ref.shape[0]), 1), fetched_ref[...]).astype(BF)
    for k in range(rels):
        prod[k] = dot(vec, rel_ref[k])
    turned[...] = vec.astype(F32).T
    for j in range(qrel_ref.shape[0]):
        kind = column(qrel_ref[j : j + 1, :])
        query = prod[0]
        for k in range(1, rels):
            query = jnp.where(kind == k, prod[k], query)
        q_ref[j * heads : (j + 1) * heads, :] = query.astype(BF)


def reversed_bits(value, count):
    return int("0" + format(value, "b").zfill(count)[::-1][:count], 2) if count else 0


def arrange(step, outer, upper, me, turned, side):
    width = turned.shape[0]
    bits = (width // step // 4).bit_length() - 1
    for at in range(width // step // 2):
        flip, line = divmod(at, 1 << bits)
        mask = upper << outer | flip << (1 - outer) | reversed_bits(line, bits) << 2
        side[at * step : (at + 1) * step, :] = turned[
            pl.ds(pl.multiple_of((me ^ mask) * step, step), step), :
        ]


def visit_kernel(step, me_ref, turned, q_ref, qrel_ref, tail_ref, ent_ref, *refs):
    blocks, refs = refs[:STOPS], refs[STOPS:]
    pw_ref, pair_ref, *sends = refs[:4]
    weights, refs = refs[4 : 4 + STOPS], refs[4 + STOPS :]
    near, weight, gq, side, load_sems, store_sems = refs
    per, heads = qrel_ref.shape
    rels = pair_ref.shape[0]
    rows = blocks[0].shape[0]
    loads = [
        pltpu.make_async_copy(block, near.at[n * rows : (n + 1) * rows], load_sems.at[n])
        for n, block in enumerate(blocks)
    ]
    for load in loads:
        load.start()
    kinds = [column(qrel_ref[j : j + 1, :]) for j in range(per)]
    for j in range(per):
        here = slice(j * heads, (j + 1) * heads)
        query = q_ref[here, :]
        tail = dot(hot(column(tail_ref[j : j + 1, :]), (heads, ent_ref.shape[0]), 1), ent_ref[...])
        score = jnp.sum(query.astype(F32) * tail, axis=1, keepdims=True)
        pw = jax.nn.sigmoid(score) - 1.0
        pw_ref[j] = pw
        gq[j] = pw * tail
    for load in loads:
        load.wait()
    stores = []
    for j in range(per):
        here = slice(j * heads, (j + 1) * heads)
        weight[here, :] = (jax.nn.sigmoid(dot_t(q_ref[here, :], near[...])) / STOPS).astype(BF)
        gq[j] = gq[j] + dot(weight[here, :], near[...])
        for n, out in enumerate(weights):
            stores.append(
                pltpu.make_async_copy(
                    weight.at[here, n * rows : (n + 1) * rows], out.at[here], store_sems.at[n, j]
                )
            )
            stores[-1].start()
    for k in range(rels):
        total = jnp.where(kinds[0] == k, gq[0], 0.0)
        for j in range(1, per):
            total = total + jnp.where(kinds[j] == k, gq[j], 0.0)
        pair_ref[k] = total.astype(BF)
    for outer, send in enumerate(sends):
        arrange(step, outer, 1, me_ref[0], turned, side)
        for k in range(send.shape[0]):
            send[k] = dot(side[...].astype(BF), pair_ref[outer * send.shape[0] + k]).astype(BF)
    for store in stores:
        store.wait()


def term_kernel(q_ref, weight_ref, term):
    term[...] = t_dot(weight_ref[...], q_ref[...]).astype(term.dtype)


def fold_kernel(parts, *refs):
    keeps, gots, refs = refs[:parts], refs[parts : 2 * parts], refs[2 * parts :]
    for n in range(parts):
        count = keeps[n].shape[0]
        rows = slice(n * count, (n + 1) * count)
        total = keeps[n][...] + gots[n][...].astype(F32)
        half = refs[0].shape[1]
        refs[0][rows] = total[:, :half]
        if len(refs) > 1:
            refs[1][rows] = total[:, half:].astype(BF)


def head_kernel(step, me_ref, pos_ref, pair_ref, rel_ref, turned, bucket_ref, keep_a, keep_b, side):
    rels, heads, _ = pair_ref.shape
    head = dot_t(pair_ref[0], rel_ref[0])
    for k in range(1, rels):
        head = head + dot_t(pair_ref[k], rel_ref[k])
    slots = bucket_ref.shape[0]
    bucket_ref[...] = dot(hot(pos_ref[...], (slots, heads), 0), head.astype(BF)).astype(BF)
    for outer, keep in enumerate((keep_a, keep_b)):
        arrange(step, outer, 0, me_ref[0], turned, side)
        for k in range(keep.shape[0]):
            keep[k] = dot(side[...].astype(BF), pair_ref[outer * keep.shape[0] + k])


def tail_kernel(tail_ref, q_ref, pw_ref, weight_ref, wanted_ref, neg_ref, returned_ref, out_ref):
    ents, heads = out_ref.shape[0], tail_ref.shape[1]
    total = jnp.zeros(out_ref.shape, F32)
    for j in range(tail_ref.shape[0]):
        spot = hot(tail_ref[j : j + 1, :], (ents, heads), 0)
        top, rest = halves(pw_ref[j] * q_ref[j * heads : (j + 1) * heads, :].astype(F32))
        total = total + dot(spot, top) + dot(spot, rest)
    spot = hot(neg_ref[...], (ents, neg_ref.shape[1]), 0)
    top, rest = halves(t_dot(weight_ref[...], q_ref[...]))
    total = total + dot(spot, top) + dot(spot, rest)
    row = as_row(wanted_column(wanted_ref))
    out_ref[...] = total + dot(hot(row, (ents, row.shape[1]), 0), returned_ref[...])


def sum_kernel(reps, me_ref, neg_ref, base_ref, *refs):
    terms = refs[: STOPS - 1]
    own_ref, outs = refs[STOPS - 1], refs[STOPS:]
    ents = base_ref.shape[0]
    total = terms[0][...].astype(F32)
    for term in terms[1:]:
        total = total + term[...].astype(F32)
    top, rest = halves(total)
    spot = hot(neg_ref[...], (ents, neg_ref.shape[1]), 0)
    full = base_ref[...] + dot(spot, top) + dot(spot, rest)
    chunk = own_ref.shape[1]
    rep = me_ref[1]
    parts = [full[:, c * chunk : (c + 1) * chunk] for c in range(reps)]

    def pick(number):
        value = parts[0]
        for c in range(1, reps):
            value = jnp.where(number == c, parts[c], value)
        return value

    own_ref[...] = pick(rep)
    for shift, out in enumerate(outs):
        out[...] = pick((rep + shift + 1) % reps).astype(BF)


def kernel(body, outs, scratch=(), smem=0, limit=VMEM, wild=0, wild_outs=0):
    def call(*args):
        count = len(args)

        def place(i):
            if i < smem:
                return pltpu.SMEM
            return pl.ANY if i >= count - wild else pltpu.VMEM

        return pl.pallas_call(
            body,
            out_shape=[o[2](*o[:2]) if len(o) > 2 else jax.ShapeDtypeStruct(*o) for o in outs],
            in_specs=[pl.BlockSpec(memory_space=place(i)) for i in range(count)],
            out_specs=[
                pl.BlockSpec(memory_space=pl.ANY if i >= len(outs) - wild_outs else pltpu.VMEM)
                for i in range(len(outs))
            ],
            scratch_shapes=[pltpu.VMEM(*s) if isinstance(s, tuple) else s for s in scratch],
            compiler_params=pltpu.CompilerParams(vmem_limit_bytes=limit),
        )(*args)

    return call


def far(value):
    return pltpu.with_memory_space_constraint(value, pltpu.HBM)


def per_device(entity, relation, head_owner, head_row, query_rel, tail_row, neg_row):
    shards, reps = lax.axis_size("blk"), lax.axis_size("rep")
    ents, width = entity.shape
    rels = relation.shape[0]
    heads = head_row.shape[0]
    per = query_rel.shape[1]
    rows = neg_row.shape[1]
    cap = max(2, 2 * heads // shards)
    slots = shards * cap
    step = width // shards
    lines = shards // 4
    me = jnp.stack([lax.axis_index("blk"), lax.axis_index("rep")]).astype(jnp.int32)

    def moved(value, distance):
        return lax.ppermute(value, "blk", [((i - distance) % shards, i) for i in range(shards)])

    def flipped(value, bit):
        return lax.ppermute(value, "blk", [(i, i ^ bit) for i in range(shards)])

    def dealt(value, groups=None):
        return lax.all_to_all(
            value, "blk", split_axis=0, concat_axis=0, tiled=True, axis_index_groups=groups
        )

    owner_row = head_owner.reshape(1, heads)
    qrel, tail = query_rel.T, tail_row.T
    (own_block,) = kernel(take_kernel, [((rows, width), BF, HM)], limit=None)(neg_row, entity)
    blocks = [own_block] + [moved(own_block, o) for o in OFFSETS]
    asked, pos = kernel(ask_kernel, [((shards, cap), jnp.int32), ((1, heads), jnp.int32)], limit=None, smem=1)(
        me, owner_row,
        head_row.reshape(1, heads),
    )
    wanted = dealt(asked)
    (served,) = kernel(
        serve_kernel,
        [((slots, width), BF, HM)],
        [((ents, width), BF), pltpu.SemaphoreType.DMA((1,))],
        wild=1,
    )(wanted, far(entity))
    fetched = dealt(served.reshape(shards, cap, width)).reshape(slots, width)

    many = per * heads
    turned, queries = kernel(
        query_kernel,
        [((width, heads), F32, VM), ((many, width), BF, VM)],
        [((rels, heads, width), F32)],
    )(pos, qrel, fetched, relation)
    part = (rels // 2, width // 2, width)
    side = ((width // 2, heads), F32)
    pos_weight, pair, send_a, send_b, *weights = kernel(
        functools.partial(visit_kernel, step),
        [((per, heads, 1), F32, HM), ((rels, heads, width), BF, VM)]
        + [(part, BF, HM)] * 2
        + [((many, rows), BF, HM)] * STOPS,
        [
            ((STOPS * rows, width), BF),
            ((many, STOPS * rows), BF),
            ((per, heads, width), F32),
            side,
            pltpu.SemaphoreType.DMA((STOPS,)),
            pltpu.SemaphoreType.DMA((STOPS, per)),
        ],
        smem=1,
        wild=STOPS,
        wild_outs=STOPS,
        limit=WIDE,
    )(me, turned, queries, qrel, tail, entity, *[far(block) for block in blocks])

    got_a = flipped(send_a, 1)
    got_b = flipped(send_b, 2)
    buckets, keep_a, keep_b = kernel(
        functools.partial(head_kernel, step),
        [((slots, width), BF, HM), (part, F32, HM), (part, F32, HM)],
        [side],
        smem=1,
    )(me, pos, pair, relation, turned)
    returned = dealt(buckets.reshape(shards, cap, width)).reshape(slots, width)
    back = []
    for n, offset in enumerate(OFFSETS):
        (term,) = kernel(term_kernel, [((rows, width), BF, HM)])(queries, weights[n + 1])
        back.append(moved(term, -offset))
    (base,) = kernel(tail_kernel, [((ents, width), F32, HM)])(
        tail, queries, pos_weight, weights[0], wanted, neg_row, returned,
    )

    def fold(keeps, gots):
        count, size = len(keeps) * keeps[0].shape[0], keeps[0].shape[1]
        outs = [((count, size, width), F32)]
        if size > step:
            outs = [((count, size // 2, width), F32), ((count, size // 2, width), BF, HM)]
        return kernel(functools.partial(fold_kernel, len(keeps)), outs)(*keeps, *gots)

    keep_a, send_a = fold([keep_a], [got_a])
    more_a = flipped(send_a, 2)
    keep_b, send_b = fold([keep_b], [got_b])
    more_b = flipped(send_b, 1)
    keep, *send = fold([keep_a, keep_b], [more_a, more_b])
    for n in range(lines.bit_length() - 1):
        got = flipped(send[0], 4 << n)
        keep, *send = fold([keep], [got])
    grad_rel = keep

    chunk = width // reps
    own, *others = kernel(
        functools.partial(sum_kernel, reps),
        [((ents, chunk), F32)] + [((ents, chunk), BF)] * (reps - 1),
        smem=1,
    )(me, neg_row, *[far(value) for value in (base, *back)])
    grad_entity = own
    for shift, other in enumerate(others):
        route = [(i, (i + shift + 1) % reps) for i in range(reps)]
        got = lax.ppermute(other, "rep", route)
        grad_entity = grad_entity + got.astype(F32)
    return (grad_entity, grad_rel)


def solution(mesh):
    placed = (
        P("blk", None),
        P("rep", None, None),
        P(("blk", "rep"), None),
        P(("blk", "rep")),
        P(("blk", "rep"), None),
        P(("blk", "rep"), None),
        P("blk", "rep"),
    )

    return jax.shard_map(
        per_device,
        mesh=mesh,
        in_specs=placed,
        out_specs=(P("blk", "rep"), P("rep", "blk", None)),
        check_vma=False,
    )
```
